32 devices in a mesh: gy: 4 (over x, core), gx: 8 (over z, y).
Axes of the slice: x: 2, y: 2, z: 4, core: 2. Of those that a mesh axis runs over, the one named last changes fastest.
Arguments:
- tokens: bfloat16 [32, 128, 384], P('gy', 'gx'), may hold values from -6 to 6
- w_qkv: bfloat16 [384, 1152], replicated, may hold values from -1 to 1
- w_out: bfloat16 [384, 384], replicated, may hold values from -0.3125 to 0.3125
- block_mask: int32 [4, 16], P('gy', 'gx'), may hold values from 0 to 1, as said below
- grad_out: bfloat16 [32, 128, 384], P('gy', 'gx'), may hold values from -6 to 6
Outputs:
- mixed: bfloat16 [32, 128, 384], P('gy', 'gx')
- d_tokens: bfloat16 [32, 128, 384], P('gy', 'gx')
The draws below stay inside these ranges and needn't reach their ends.
Inputs may be any that keep to these rules, and one draw needn't show every extreme that they name: `block_mask`: 1 marks a tissue block, 0 background.
All inputs are finite; a program needn't handle non-finite values.
Results may differ from the reference program's by a relative error of at most 0.017.
Values may be sent and summed in bfloat16 or wider, within the bound.
No kernel may reach another device: no remote copies, remote signals or barrier semaphores. Data moves between devices by JAX's collectives and lax.ppermute only.
A program may use at most 64 MiB of HBM per device.

```python
import jax
import jax.numpy as jnp
from jax import lax

NH = 6
HEAD_SIZE = 64
KS = 7
TISSUE_BLOCK = 8
TH = 8
TW = 16
C = 384
H = 32
W = 128
N_GY = 4
N_GX = 8


def draw_block_mask(key, part):
    block_rows = H // TISSUE_BLOCK
    block_cols = W // TISSUE_BLOCK
    tile_brows = TH // TISSUE_BLOCK
    tile_bcols = TW // TISSUE_BLOCK
    levels = jax.random.randint(jax.random.fold_in(key, 11), (block_rows // tile_brows, block_cols // tile_bcols), 4, 13)
    levels = jnp.repeat(jnp.repeat(levels, tile_brows, 0), tile_bcols, 1)
    picks = jax.random.randint(jax.random.fold_in(key, 12), (block_rows, block_cols), 0, 16)
    return (picks < levels).astype(jnp.int32)


def draw_tokens(key, part):
    block_rows = H // TISSUE_BLOCK
    block_cols = W // TISSUE_BLOCK
    width = NH * HEAD_SIZE
    shared = jax.random.normal(jax.random.fold_in(key, 21), (block_rows, block_cols, width), jnp.float32)
    noise = jax.random.normal(jax.random.fold_in(key, 22), (H, W, width), jnp.float32)
    field = 0.2 * jnp.repeat(jnp.repeat(shared, TISSUE_BLOCK, 0), TISSUE_BLOCK, 1) + 0.98 * noise
    field = jnp.clip(field, -6.0, 6.0)
    return field.astype(jnp.bfloat16)


def draw_w_qkv(key, part):
    width = NH * HEAD_SIZE
    factor = width ** (-0.5)
    whole = jax.random.truncated_normal(jax.random.fold_in(key, 31), -3.0, 3.0, (width, 3 * width), jnp.float32) * factor
    return whole.astype(jnp.bfloat16)


def steps_of(key, shape, pieces, least, top_value):
    level = 1.0
    for position, blocks in pieces:
        draws = jax.random.uniform(jax.random.fold_in(jax.random.fold_in(key, 6), position), (blocks,), jnp.float32, least / len(pieces), top_value / len(pieces))
        level = level * jnp.repeat(jnp.exp(draws), shape[position] // blocks).reshape((-1,) + (1,) * (len(shape) - 1 - position))
    return level


def gaussian(key, extent, scale, most, split=(), kind=jnp.bfloat16):
    drawn = jax.random.normal(key, extent, jnp.float32) * scale
    if len(split) > 0:
        drawn = steps_of(key, extent, split, -0.22, 0.18) * drawn
    return jnp.clip(drawn, min=-most, max=most).astype(kind)


def setup_inputs(seed: int = 0) -> dict:
    splits = jax.random.split(jax.random.key(seed), 6)
    return {
        "tokens": draw_tokens(jax.random.fold_in(splits[5], 71), 0),
        "w_qkv": draw_w_qkv(jax.random.fold_in(splits[5], 71), 0),
        "w_out": gaussian(splits[2], (C, C), C ** -0.5, 0.3125),
        "block_mask": draw_block_mask(jax.random.fold_in(splits[5], 71), 0),
        "grad_out": gaussian(splits[4], (H, W, C), 1.0, 6.0, ((0, 4), (1, 8))),
    }


NEG_FILL = -1e30


def broadcast_blocks(blocks):
    return jnp.repeat(jnp.repeat(blocks, TISSUE_BLOCK, 0), TISSUE_BLOCK, 1)


def reference(tokens, w_qkv, w_out, block_mask, grad_out):
    region_height, region_width, width = tokens.shape
    reachable_cells = KS // 2
    score_scale = HEAD_SIZE ** -0.5
    flat_tokens = tokens.reshape(-1, width)
    qkv = jnp.dot(flat_tokens, w_qkv, preferred_element_type=jnp.float32).astype(jnp.bfloat16)
    token_flag = broadcast_blocks(block_mask).astype(jnp.float32).reshape(-1, 1)
    d_att = (jnp.dot(grad_out.reshape(-1, width), w_out.T, preferred_element_type=jnp.float32) * token_flag).astype(jnp.bfloat16)

    def split_heads(field):
        return field.reshape(region_height, region_width, NH, HEAD_SIZE).transpose(2, 0, 1, 3)

    query_all = split_heads(qkv[:, :width])
    keys_all = split_heads(qkv[:, width:2 * width])
    values_all = split_heads(qkv[:, 2 * width:])
    datt_all = split_heads(d_att)
    inside = jnp.pad(jnp.ones((region_height, region_width), bool), reachable_cells)
    pool_ok = block_mask > 0
    row_flag = pool_ok.reshape(N_GY, -1)
    col_flag = pool_ok.reshape(region_height // TISSUE_BLOCK, N_GX, TW // TISSUE_BLOCK).transpose(1, 0, 2).reshape(N_GX, -1)
    shifts = [(row_off, col_off) for row_off in range(-reachable_cells, reachable_cells + 1) for col_off in range(-reachable_cells, reachable_cells + 1)]

    def to_rows(field):
        return field.reshape(N_GY, TH * region_width, field.shape[-1])

    def from_rows(field):
        return field.reshape(region_height, region_width, field.shape[-1])

    def to_cols(field):
        return field.reshape(region_height, N_GX, TW, field.shape[-1]).transpose(1, 0, 2, 3).reshape(N_GX, region_height * TW, field.shape[-1])

    def from_cols(field):
        return field.reshape(N_GX, region_height, TW, field.shape[-1]).transpose(1, 0, 2, 3).reshape(region_height, region_width, field.shape[-1])

    def pool_blocks(field):
        grouped = field.astype(jnp.float32).reshape(region_height // TISSUE_BLOCK, TISSUE_BLOCK, region_width // TISSUE_BLOCK, TISSUE_BLOCK, HEAD_SIZE)
        return (jnp.sum(grouped, axis=(1, 3)) / TISSUE_BLOCK).astype(jnp.bfloat16)

    def col_pack(blocks):
        return blocks.reshape(region_height // TISSUE_BLOCK, N_GX, TW // TISSUE_BLOCK, HEAD_SIZE).transpose(1, 0, 2, 3).reshape(N_GX, -1, HEAD_SIZE)

    def col_unpack(blocks):
        return blocks.reshape(N_GX, region_height // TISSUE_BLOCK, TW // TISSUE_BLOCK, HEAD_SIZE).transpose(1, 0, 2, 3).reshape(region_height // TISSUE_BLOCK, region_width // TISSUE_BLOCK, HEAD_SIZE)

    def window(field, row_off, col_off):
        return field[reachable_cells + row_off:reachable_cells + row_off + region_height, reachable_cells + col_off:reachable_cells + col_off + region_width]

    def one_head(operands):
        query_h, keys_h, values_h, datt_h = operands
        query_f = query_h.astype(jnp.float32)
        attention_grad_flat = datt_h.astype(jnp.float32)
        pad_spec = ((reachable_cells, reachable_cells), (reachable_cells, reachable_cells), (0, 0))
        keys_pad = jnp.pad(keys_h, pad_spec)
        values_pad = jnp.pad(values_h, pad_spec)
        local_s = jnp.stack([jnp.where(window(inside, ro, co), jnp.sum(query_f * window(keys_pad, ro, co).astype(jnp.float32), -1) * score_scale, NEG_FILL) for ro, co in shifts])
        pooled_k = pool_blocks(keys_h)
        pooled_v = pool_blocks(values_h)
        row_keys = pooled_k.reshape(N_GY, -1, HEAD_SIZE).astype(jnp.float32)
        row_vals = pooled_v.reshape(N_GY, -1, HEAD_SIZE).astype(jnp.float32)
        col_keys = col_pack(pooled_k).astype(jnp.float32)
        col_vals = col_pack(pooled_v).astype(jnp.float32)
        row_s = jnp.einsum("gtd,gpd->gtp", to_rows(query_f), row_keys) * score_scale
        row_s = from_rows(jnp.where(row_flag[:, None, :], row_s, NEG_FILL))
        col_s = jnp.einsum("gtd,gpd->gtp", to_cols(query_f), col_keys) * score_scale
        col_s = from_cols(jnp.where(col_flag[:, None, :], col_s, NEG_FILL))
        top = jnp.maximum(jnp.maximum(jnp.max(local_s, 0), jnp.max(row_s, -1)), jnp.max(col_s, -1))
        total = jnp.sum(jnp.exp(local_s - top), 0) + jnp.sum(jnp.exp(row_s - top[..., None]), -1) + jnp.sum(jnp.exp(col_s - top[..., None]), -1)
        lse = top + jnp.log(total)
        local_probs = jnp.exp(local_s - lse)
        row_pf = jnp.exp(row_s - lse[..., None])
        col_pf = jnp.exp(col_s - lse[..., None])
        row_ph = row_pf.astype(jnp.bfloat16).astype(jnp.float32)
        col_ph = col_pf.astype(jnp.bfloat16).astype(jnp.float32)
        output = jnp.zeros((region_height, region_width, HEAD_SIZE), jnp.float32)
        for position_index, (ro, co) in enumerate(shifts):
            output = output + local_probs[position_index][..., None] * window(values_pad, ro, co).astype(jnp.float32)
        output = output + from_rows(jnp.einsum("gtp,gpd->gtd", to_rows(row_ph), row_vals))
        output = output + from_cols(jnp.einsum("gtp,gpd->gtd", to_cols(col_ph), col_vals))
        out_half = output.astype(jnp.bfloat16)
        delta = jnp.sum(attention_grad_flat * out_half.astype(jnp.float32), -1)
        grad_q = jnp.zeros((region_height, region_width, HEAD_SIZE), jnp.float32)
        grad_kpad = jnp.zeros((region_height + 2 * reachable_cells, region_width + 2 * reachable_cells, HEAD_SIZE), jnp.float32)
        padded_value_gradient = jnp.zeros((region_height + 2 * reachable_cells, region_width + 2 * reachable_cells, HEAD_SIZE), jnp.float32)
        for position_index, (ro, co) in enumerate(shifts):
            key_win = window(keys_pad, ro, co).astype(jnp.float32)
            value_win = window(values_pad, ro, co).astype(jnp.float32)
            prob_grad = jnp.sum(attention_grad_flat * value_win, -1)
            score_grad = local_probs[position_index] * (prob_grad - delta)
            grad_q = grad_q + score_grad[..., None] * key_win * score_scale
            row_extent = slice(reachable_cells + ro, reachable_cells + ro + region_height)
            column_extent = slice(reachable_cells + co, reachable_cells + co + region_width)
            grad_kpad = grad_kpad.at[row_extent, column_extent].add(score_grad[..., None] * query_f * score_scale)
            padded_value_gradient = padded_value_gradient.at[row_extent, column_extent].add(local_probs[position_index][..., None] * attention_grad_flat)
        row_dp = jnp.einsum("gtd,gpd->gtp", to_rows(attention_grad_flat), row_vals)
        row_ds = (to_rows(row_pf) * (row_dp - to_rows(delta[..., None]))).astype(jnp.bfloat16).astype(jnp.float32)
        col_dp = jnp.einsum("gtd,gpd->gtp", to_cols(attention_grad_flat), col_vals)
        col_ds = (to_cols(col_pf) * (col_dp - to_cols(delta[..., None]))).astype(jnp.bfloat16).astype(jnp.float32)
        grad_q = grad_q + from_rows(jnp.einsum("gtp,gpd->gtd", row_ds, row_keys)) * score_scale
        grad_q = grad_q + from_cols(jnp.einsum("gtp,gpd->gtd", col_ds, col_keys)) * score_scale
        row_gk = jnp.einsum("gtp,gtd->gpd", row_ds, to_rows(query_f)) * score_scale
        row_gv = jnp.einsum("gtp,gtd->gpd", to_rows(row_ph), to_rows(attention_grad_flat))
        col_gk = jnp.einsum("gtp,gtd->gpd", col_ds, to_cols(query_f)) * score_scale
        col_gv = jnp.einsum("gtp,gtd->gpd", to_cols(col_ph), to_cols(attention_grad_flat))
        block_gk = row_gk.reshape(region_height // TISSUE_BLOCK, region_width // TISSUE_BLOCK, HEAD_SIZE) + col_unpack(col_gk)
        block_value_grads = row_gv.reshape(region_height // TISSUE_BLOCK, region_width // TISSUE_BLOCK, HEAD_SIZE) + col_unpack(col_gv)
        trimmed_region = (slice(reachable_cells, reachable_cells + region_height), slice(reachable_cells, reachable_cells + region_width))
        grad_k = grad_kpad[trimmed_region] + broadcast_blocks(block_gk / TISSUE_BLOCK)
        value_gradient = padded_value_gradient[trimmed_region] + broadcast_blocks(block_value_grads / TISSUE_BLOCK)
        return out_half, grad_q, grad_k, value_gradient

    out_all, grad_q_all, grad_k_all, grad_v_all = lax.map(one_head, (query_all, keys_all, values_all, datt_all))

    def merge_heads(field):
        return field.transpose(1, 2, 0, 3).reshape(region_height * region_width, width)

    attended = merge_heads(out_all)
    gated = attended * token_flag.astype(jnp.bfloat16)
    mixed = (flat_tokens.astype(jnp.float32) + jnp.dot(gated, w_out, preferred_element_type=jnp.float32)).astype(jnp.bfloat16)
    d_qkv = jnp.concatenate([merge_heads(grad_q_all), merge_heads(grad_k_all), merge_heads(grad_v_all)], 1).astype(jnp.bfloat16)
    d_tokens = (grad_out.reshape(-1, width).astype(jnp.float32) + jnp.dot(d_qkv, w_qkv.T, preferred_element_type=jnp.float32)).astype(jnp.bfloat16)
    return mixed.reshape(region_height, region_width, width), d_tokens.reshape(region_height, region_width, width)
```

```python
import functools

import jax
import jax.numpy as jnp
import numpy as np
from jax import lax
from jax.experimental import pallas as pl
from jax.experimental.pallas import tpu as pltpu
from jax.sharding import PartitionSpec as P

NH = 6
HEAD_SIZE = 64
KS = 7
TISSUE_BLOCK = 8
REACH = KS // 2
NEG_FILL = -1e30
LANES = 128


def pairs_low(count):
    return [(i, i ^ 1) for i in range(count)]


def pairs_odd(count, wrap):
    moves = []
    for i in range(count):
        j = (i + 1) % count if i % 2 else (i - 1) % count
        if wrap or abs(i - j) == 1:
            moves.append((i, j))
    return moves


def pairs_far(count, step):
    return [(i, i ^ step) for i in range(count)]


def window_pairs(count, step):
    moves = []
    for i in range(count):
        group, side = divmod((i - 1) % count, 2)
        moves.append((i, (2 * (group ^ step) + 1 + side) % count))
    return moves


def steps_above(count, first):
    steps = []
    while first < count:
        steps.append(first)
        first *= 2
    return steps


class Rows:
    def __init__(self, tile_rows, tile_cols, pooled):
        wide = tile_cols + 2 * REACH
        self.own = tile_rows * tile_cols
        self.side = tile_rows * REACH
        self.edge = REACH * wide
        self.left = self.own
        self.right = self.left + self.side
        self.up = self.right + self.side
        self.down = self.up + self.edge
        self.local = self.down + self.edge
        self.pool = -(-self.local // 16) * 16
        self.used = self.pool + pooled
        self.total = -(-self.used // LANES) * LANES


def band_table(rows, tile_rows, tile_cols):
    wide = tile_cols + 2 * REACH
    place = np.full((rows.total, 2), -1000, np.int64)
    own = np.stack(np.meshgrid(np.arange(tile_rows), np.arange(tile_cols), indexing="ij"), -1).reshape(-1, 2)
    side = np.stack(np.meshgrid(np.arange(tile_rows), np.arange(REACH), indexing="ij"), -1).reshape(-1, 2)
    edge = np.stack(np.meshgrid(np.arange(REACH), np.arange(wide), indexing="ij"), -1).reshape(-1, 2)
    place[: rows.own] = own
    place[rows.left : rows.right] = side + [0, -REACH]
    place[rows.right : rows.up] = side + [0, tile_cols]
    place[rows.up : rows.down] = edge + [-REACH, -REACH]
    place[rows.down : rows.local] = edge + [tile_rows, -REACH]
    near = (np.abs(place[:, None, :] - own[None, :, :]) <= REACH).all(-1)
    band = np.where(near, 0.0, NEG_FILL).astype(np.float32)
    cols = np.broadcast_to(place[:, 1:2], band.shape).astype(np.int32)
    return band, cols


def attention_kernel(
    rows, tile_cols, sizes,
    mask_ref, x_ref, flags_ref, band_ref, cols_ref, grad_ref, wqkv_ref, wout_ref,
    mixed_ref, back_ref, dkv_ref, att_ref, dq_ref,
):
    width = NH * HEAD_SIZE
    own = rows.own
    count_y, count_x = sizes
    iy, ix = lax.axis_index("gy"), lax.axis_index("gx")
    dot = functools.partial(lax.dot_general, preferred_element_type=jnp.float32)
    nn = (((1,), (0,)), ((), ()))
    nt = (((1,), (1,)), ((), ()))

    row_id = lax.broadcasted_iota(jnp.int32, (rows.total, own), 0)
    cols = cols_ref[...]
    local_row = row_id < rows.pool
    outside = (
        ((cols < 0) & (ix == 0) & local_row)
        | ((cols >= tile_cols) & (ix == count_x - 1))
        | ((row_id >= rows.up) & (row_id < rows.down) & (iy == 0))
        | ((row_id >= rows.down) & (row_id < rows.local) & (iy == count_y - 1))
    )
    bias = jnp.where(outside, NEG_FILL, band_ref[...])
    pooled = jnp.where(flags_ref[...] > 0, 0.0, NEG_FILL)
    bias = jnp.concatenate([bias[: rows.pool], pooled], axis=0)
    bias2 = jnp.concatenate([bias, bias], axis=1)

    token = lax.broadcasted_iota(jnp.int32, (own, width), 0)
    block_cols = tile_cols // TISSUE_BLOCK
    block = token // (tile_cols * TISSUE_BLOCK) * block_cols + token % tile_cols // TISSUE_BLOCK
    flag = jnp.zeros((own, width), jnp.float32)
    for b in range(mask_ref.shape[0] * mask_ref.shape[1]):
        value = mask_ref[b // block_cols, b % block_cols].astype(jnp.float32)
        flag = jnp.where(block == b, value, flag)

    x = x_ref[...]
    tokens = x[:own]
    kv = dot(x, wqkv_ref[:, width:], nn).astype(jnp.bfloat16)
    keys, values = kv[:, :width], kv[:, width:]
    scale = HEAD_SIZE**-0.5
    query = (dot(tokens, wqkv_ref[:, :width], nn).astype(jnp.bfloat16).astype(jnp.float32) * scale).astype(jnp.bfloat16)
    d_att = (dot(grad_ref[...], wout_ref[...], nt) * flag).astype(jnp.bfloat16)
    keys_t, values_t, d_att_t = keys.T, values.T, d_att.T
    low = lax.broadcasted_iota(jnp.int32, (own, LANES), 1) < HEAD_SIZE
    none = jnp.zeros((own, LANES), jnp.bfloat16)

    for pair in range(width // LANES):
        lanes = slice(pair * LANES, (pair + 1) * LANES)
        heads = [slice(pair * LANES + h * HEAD_SIZE, pair * LANES + (h + 1) * HEAD_SIZE) for h in range(2)]
        k_pair, v_pair = keys[:, lanes], values[:, lanes]
        q_pair, d_pair = query[:, lanes], d_att[:, lanes]
        q_two = jnp.concatenate([jnp.where(low, q_pair, none), jnp.where(low, none, q_pair)], axis=0)
        d_two = jnp.concatenate([jnp.where(low, d_pair, none), jnp.where(low, none, d_pair)], axis=0)
        scores = dot(k_pair, q_two, nt) + bias2
        top = jnp.max(scores, axis=0, keepdims=True)
        raised = jnp.exp(scores - top)
        prob = raised * (1.0 / jnp.sum(raised, axis=0, keepdims=True))
        prob_half = prob.astype(jnp.bfloat16)
        deltas = []
        for h, head in enumerate(heads):
            part = dot(values_t[head], prob_half[:, h * own : (h + 1) * own], nn).astype(jnp.bfloat16)
            att_ref[head] = part
            deltas.append(
                jnp.sum(d_att_t[head].astype(jnp.float32) * part.astype(jnp.float32), axis=0, keepdims=True)
            )
        delta = jnp.concatenate(deltas, axis=1)
        prob_grad = dot(v_pair, d_two, nt)
        score_grad = (prob * (prob_grad - delta)).astype(jnp.bfloat16)
        dkv_ref[:, lanes] = dot(score_grad, q_two, nn).astype(jnp.bfloat16)
        dkv_ref[:, width + pair * LANES : width + (pair + 1) * LANES] = dot(prob_half, d_two, nn).astype(jnp.bfloat16)
        for h, head in enumerate(heads):
            part = dot(keys_t[head], score_grad[:, h * own : (h + 1) * own], nn) * scale
            dq_ref[head] = part.astype(jnp.bfloat16)

    attended = (att_ref[...].T.astype(jnp.float32) * flag).astype(jnp.bfloat16)
    mixed_ref[...] = (tokens.astype(jnp.float32) + dot(attended, wout_ref[...], nn)).astype(jnp.bfloat16)
    back = dot(dkv_ref[...], wqkv_ref[:, width:], nt)
    d_query = dq_ref[...].T
    back_ref[:own] = back[:own] + grad_ref[...].astype(jnp.float32) + dot(d_query, wqkv_ref[:, :width], nt)
    back_ref[own:] = back[own:]


def attend(rows, tile_cols, sizes, block_mask, x_all, flags, grad_flat, w_qkv, w_out):
    width = x_all.shape[1]
    band, cols = band_table(rows, rows.own // tile_cols, tile_cols)
    vmem = pl.BlockSpec(memory_space=pltpu.VMEM)
    return pl.pallas_call(
        functools.partial(attention_kernel, rows, tile_cols, sizes),
        out_shape=(
            jax.ShapeDtypeStruct((rows.own, width), jnp.bfloat16),
            jax.ShapeDtypeStruct((rows.total, width), jnp.float32),
        ),
        in_specs=[pl.BlockSpec(memory_space=pltpu.SMEM)] + [vmem] * 7,
        out_specs=(vmem, vmem),
        scratch_shapes=[
            pltpu.VMEM((rows.total, 2 * width), jnp.bfloat16),
            pltpu.VMEM((width, rows.own), jnp.bfloat16),
            pltpu.VMEM((width, rows.own), jnp.bfloat16),
        ],
        compiler_params=pltpu.CompilerParams(vmem_limit_bytes=48 << 20),
        name="attention",
    )(block_mask, x_all, flags, jnp.asarray(band), jnp.asarray(cols), grad_flat, w_qkv, w_out)


def local(tokens, w_qkv, w_out, block_mask, grad_out):
    tile_rows, tile_cols, width = tokens.shape
    count_y, count_x = lax.axis_size("gy"), lax.axis_size("gx")
    blocks = block_mask.shape[0] * block_mask.shape[1]
    rows = Rows(tile_rows, tile_cols, blocks * (count_y + count_x))
    side, edge, wide = rows.side, rows.edge, tile_cols + 2 * REACH
    even_y, even_x = lax.axis_index("gy") % 2 == 0, lax.axis_index("gx") % 2 == 0
    flat_tokens = tokens.reshape(rows.own, width)
    grad_flat = grad_out.reshape(rows.own, width)

    grouped = tokens.astype(jnp.float32).reshape(
        tile_rows // TISSUE_BLOCK, TISSUE_BLOCK, tile_cols // TISSUE_BLOCK, TISSUE_BLOCK, width
    )
    sums = (jnp.sum(grouped, axis=(1, 3)) / TISSUE_BLOCK).reshape(blocks, width).astype(jnp.bfloat16)
    marks = jnp.broadcast_to(block_mask.reshape(blocks, 1), (blocks, width)).astype(jnp.bfloat16)
    mine = jnp.concatenate([sums, marks], axis=0)
    first = tokens[:, :REACH].reshape(side, width)
    last = tokens[:, tile_cols - REACH :].reshape(side, width)
    low_x = lax.ppermute(
        jnp.concatenate([jnp.where(even_x, last, first), mine], axis=0), "gx", pairs_low(count_x)
    )
    odd_x = lax.ppermute(jnp.where(even_x, first, last), "gx", pairs_odd(count_x, False))
    left = jnp.where(even_x, odd_x, low_x[:side])
    right = jnp.where(even_x, low_x[:side], odd_x)
    row_pool = jnp.concatenate([mine, low_x[side:]], axis=0)
    for step in steps_above(count_x, 2):
        row_pool = jnp.concatenate([row_pool, lax.ppermute(row_pool, "gx", pairs_far(count_x, step))], axis=0)
    spread = jnp.concatenate(
        [left.reshape(tile_rows, REACH, width), tokens, right.reshape(tile_rows, REACH, width)], axis=1
    )
    top, bottom = spread[:REACH].reshape(edge, width), spread[tile_rows - REACH :].reshape(edge, width)
    low_y = lax.ppermute(
        jnp.concatenate([jnp.where(even_y, bottom, top), mine], axis=0), "gy", pairs_low(count_y)
    )
    odd_y = lax.ppermute(
        jnp.concatenate([jnp.where(even_y, top, bottom), mine, low_y[edge:]], axis=0), "gy", pairs_odd(count_y, True)
    )
    up = jnp.where(even_y, odd_y[:edge], low_y[:edge])
    down = jnp.where(even_y, low_y[:edge], odd_y[:edge])
    col_pool = jnp.concatenate([mine, low_y[edge:], odd_y[edge:]], axis=0)
    for step in steps_above(count_y // 2, 2):
        col_pool = jnp.concatenate([col_pool, lax.ppermute(col_pool, "gy", window_pairs(count_y, step))], axis=0)
    pool = jnp.concatenate([row_pool, col_pool], axis=0).reshape(count_x + count_y, 2, blocks, width)
    x_all = jnp.concatenate(
        [
            flat_tokens,
            left,
            right,
            up,
            down,
            jnp.zeros((rows.pool - rows.local, width), jnp.bfloat16),
            pool[:, 0].reshape(-1, width),
            jnp.zeros((rows.total - rows.used, width), jnp.bfloat16),
        ],
        axis=0,
    )
    flags = pool[:, 1, :, : rows.own].reshape(-1, rows.own).astype(jnp.float32)
    flags = jnp.concatenate([flags, jnp.zeros((rows.total - rows.used, rows.own), jnp.float32)], axis=0)

    mixed, back = attend(rows, tile_cols, (count_y, count_x), block_mask, x_all, flags, grad_flat, w_qkv, w_out)

    half = jnp.bfloat16
    row_grad = back[rows.pool : rows.pool + count_x * blocks]
    col_grad = back[rows.pool + count_x * blocks : rows.used]

    def fold(grads, axis, moves):
        middle = grads.shape[0] // 2
        return grads[:middle] + lax.ppermute(grads[middle:].astype(half), axis, moves).astype(jnp.float32)

    for step in reversed(steps_above(count_x, 2)):
        row_grad = fold(row_grad, "gx", pairs_far(count_x, step))
    for step in reversed(steps_above(count_y // 2, 2)):
        col_grad = fold(col_grad, "gy", window_pairs(count_y, step))
    up_back, down_back = back[rows.up : rows.down], back[rows.down : rows.local]
    got = lax.ppermute(
        jnp.concatenate([jnp.where(even_y, up_back, down_back), col_grad[2 * blocks :]], axis=0).astype(half),
        "gy",
        pairs_odd(count_y, True),
    ).astype(jnp.float32)
    odd_back = got[:edge].reshape(REACH, wide, width)
    col_grad = col_grad[: 2 * blocks] + got[edge:]
    got = lax.ppermute(
        jnp.concatenate([jnp.where(even_y, down_back, up_back), col_grad[blocks:]], axis=0).astype(half),
        "gy",
        pairs_low(count_y),
    ).astype(jnp.float32)
    low_back = got[:edge].reshape(REACH, wide, width)
    block_grad = col_grad[:blocks] + got[edge:]
    spread_back = jnp.concatenate(
        [
            back[rows.left : rows.right].reshape(tile_rows, REACH, width),
            back[: rows.own].reshape(tile_rows, tile_cols, width),
            back[rows.right : rows.up].reshape(tile_rows, REACH, width),
        ],
        axis=1,
    )
    top_back = jnp.where(even_y, odd_back, low_back)
    bottom_back = jnp.where(even_y, low_back, odd_back)
    spread_back = spread_back + jnp.pad(top_back, ((0, tile_rows - REACH), (0, 0), (0, 0)))
    spread_back = spread_back + jnp.pad(bottom_back, ((tile_rows - REACH, 0), (0, 0), (0, 0)))
    left_back = spread_back[:, :REACH].reshape(side, width)
    right_back = spread_back[:, REACH + tile_cols :].reshape(side, width)
    odd_got = lax.ppermute(
        jnp.where(even_x, left_back, right_back).astype(half), "gx", pairs_odd(count_x, False)
    ).astype(jnp.float32)
    low_got = lax.ppermute(
        jnp.concatenate([jnp.where(even_x, right_back, left_back), row_grad[blocks:]], axis=0).astype(half),
        "gx",
        pairs_low(count_x),
    ).astype(jnp.float32)
    block_grad = block_grad + row_grad[:blocks] + low_got[side:]
    first_back = jnp.where(even_x, odd_got, low_got[:side]).reshape(tile_rows, REACH, width)
    last_back = jnp.where(even_x, low_got[:side], odd_got).reshape(tile_rows, REACH, width)
    d_tokens = spread_back[:, REACH : REACH + tile_cols]
    d_tokens = d_tokens + jnp.pad(first_back, ((0, 0), (0, tile_cols - REACH), (0, 0)))
    d_tokens = d_tokens + jnp.pad(last_back, ((0, 0), (tile_cols - REACH, 0), (0, 0)))
    shaped = (block_grad / TISSUE_BLOCK).reshape(tile_rows // TISSUE_BLOCK, tile_cols // TISSUE_BLOCK, width)
    d_tokens = d_tokens + jnp.repeat(jnp.repeat(shaped, TISSUE_BLOCK, 0), TISSUE_BLOCK, 1)
    return mixed.reshape(tile_rows, tile_cols, width), d_tokens.astype(jnp.bfloat16)


def solution(mesh):
    placed = (P("gy", "gx", None), P(), P(), P("gy", "gx"), P("gy", "gx", None))
    return jax.shard_map(
        local,
        mesh=mesh,
        in_specs=placed,
        out_specs=(P("gy", "gx", None), P("gy", "gx", None)),
        check_vma=False,
    )
```

```python
import functools

import jax
import jax.numpy as jnp
import numpy as np
from jax import lax
from jax.experimental import pallas as pl
from jax.experimental.pallas import tpu as pltpu
from jax.sharding import PartitionSpec as P

NH = 6
HEAD_SIZE = 64
KS = 7
TISSUE_BLOCK = 8
REACH = KS // 2
NEG_FILL = -1e30
LANES = 128
ALIGN = 16
FAR = -1000


def pairs_low(count):
    return [(i, i ^ 1) for i in range(count)]


def pairs_odd(count, wrap):
    moves = []
    for i in range(count):
        j = (i + 1) % count if i % 2 else (i - 1) % count
        if wrap or abs(i - j) == 1:
            moves.append((i, j))
    return moves


def pairs_far(count, step):
    return [(i, i ^ step) for i in range(count)]


def window_pairs(count, step):
    moves = []
    for i in range(count):
        group, side = divmod((i - 1) % count, 2)
        moves.append((i, (2 * (group ^ step) + 1 + side) % count))
    return moves


def steps_above(count, first):
    steps = []
    while first < count:
        steps.append(first)
        first *= 2
    return steps


def padded(count, unit=ALIGN):
    return -(-count // unit) * unit


class Rows:
    def __init__(self, tile_rows, tile_cols, pooled):
        self.tile_rows, self.tile_cols = tile_rows, tile_cols
        self.wide = tile_cols + 2 * REACH
        self.own = tile_rows * tile_cols
        self.side = tile_rows * REACH
        self.edge = REACH * self.wide
        self.low_x = self.own
        self.odd_x = self.low_x + padded(self.side)
        self.low_y = self.odd_x + padded(self.side)
        self.odd_y = self.low_y + padded(self.edge)
        self.pool = self.odd_y + padded(self.edge)
        self.pooled = pooled
        self.used = self.pool + pooled
        self.total = padded(self.used, LANES)


def places(rows):
    tile_rows, tile_cols = rows.tile_rows, rows.tile_cols
    place = np.full((2, 2, rows.total, 2), FAR, np.int32)

    def grid(first, second):
        return np.stack(np.meshgrid(np.asarray(first), np.asarray(second), indexing="ij"), -1).reshape(-1, 2)

    before, own_cols, after = np.arange(-REACH, 0), np.arange(tile_cols), tile_cols + np.arange(REACH)
    above, own_rows, below = np.arange(-REACH, 0), np.arange(tile_rows), tile_rows + np.arange(REACH)
    for odd_y in range(2):
        for odd_x in range(2):
            low_cols, odd_cols = (before, after) if odd_x else (after, before)
            low_rows, odd_rows = (above, below) if odd_y else (below, above)
            wide_cols = np.concatenate([low_cols, own_cols, odd_cols])
            spot = place[odd_y, odd_x]
            spot[: rows.own] = grid(own_rows, own_cols)
            spot[rows.low_x : rows.low_x + rows.side] = grid(own_rows, low_cols)
            spot[rows.odd_x : rows.odd_x + rows.side] = grid(own_rows, odd_cols)
            spot[rows.low_y : rows.low_y + rows.edge] = grid(low_rows, wide_cols)
            spot[rows.odd_y : rows.odd_y + rows.edge] = grid(odd_rows, wide_cols)
    return place


def window_bias(rows, count_y, count_x):
    iy, ix = lax.axis_index("gy"), lax.axis_index("gx")
    table = jnp.asarray(places(rows))
    key = table[iy % 2, ix % 2]
    key_row, key_col = key[:, :1], key[:, 1:]
    token = np.arange(rows.own)[None, :]
    near = (jnp.abs(key_row - token // rows.tile_cols) <= REACH) & (jnp.abs(key_col - token % rows.tile_cols) <= REACH)
    row, col = iy * rows.tile_rows + key_row, ix * rows.tile_cols + key_col
    inside = (row >= 0) & (row < count_y * rows.tile_rows) & (col >= 0) & (col < count_x * rows.tile_cols)
    return jnp.where(near & inside, 0.0, NEG_FILL).astype(jnp.float32)


DOT = functools.partial(lax.dot_general, preferred_element_type=jnp.float32)
NN = (((1,), (0,)), ((), ()))
NT = (((1,), (1,)), ((), ()))
SCALE = HEAD_SIZE**-0.5


def token_flags(rows, mask_ref, width):
    token = lax.broadcasted_iota(jnp.int32, (rows.own, width), 0)
    block_cols = rows.tile_cols // TISSUE_BLOCK
    block = token // (rows.tile_cols * TISSUE_BLOCK) * block_cols + token % rows.tile_cols // TISSUE_BLOCK
    flag = jnp.zeros((rows.own, width), jnp.float32)
    for b in range(mask_ref.shape[0] * mask_ref.shape[1]):
        value = mask_ref[b // block_cols, b % block_cols].astype(jnp.float32)
        flag = jnp.where(block == b, value, flag)
    return flag


def own_kernel(rows, mask_ref, tokens_ref, grad_ref, wqkv_ref, wout_ref, query_ref, kv_ref, datt_ref):
    width = NH * HEAD_SIZE
    tokens = tokens_ref[...]
    query = DOT(tokens, wqkv_ref[:, :width], NN).astype(jnp.bfloat16).astype(jnp.float32) * SCALE
    query_ref[...] = query.astype(jnp.bfloat16)
    kv_ref[...] = DOT(tokens, wqkv_ref[:, width:], NN).astype(jnp.bfloat16)
    flag = token_flags(rows, mask_ref, width)
    datt_ref[...] = (DOT(grad_ref[...], wout_ref[...], NT) * flag).astype(jnp.bfloat16)


def attention_kernel(
    rows,
    low_x_ref, odd_x_ref, low_y_ref, odd_y_ref, pool_ref, flags_ref, bias_ref, query_ref, kv_ref, datt_ref, wkv_ref,
    back_ref, dkv_ref, att_ref, dq_ref,
    x_ref, all_kv_ref, all_dkv_ref,
):
    width = NH * HEAD_SIZE
    own = rows.own
    pooled = jnp.where(flags_ref[...] > 0, 0.0, NEG_FILL)
    bias = jnp.concatenate([bias_ref[: rows.pool], pooled], axis=0)
    bias2 = jnp.concatenate([bias, bias], axis=1)

    x_ref[...] = jnp.zeros_like(x_ref)
    for start, ref, count in (
        (rows.low_x, low_x_ref, rows.side),
        (rows.odd_x, odd_x_ref, rows.side),
        (rows.low_y, low_y_ref, rows.edge),
        (rows.odd_y, odd_y_ref, rows.edge),
        (rows.pool, pool_ref, rows.total - rows.pool),
    ):
        x_ref[start - own : start - own + count] = ref[:count]
    all_kv_ref[:own] = kv_ref[...]
    all_kv_ref[own:] = DOT(x_ref[...], wkv_ref[...], NN).astype(jnp.bfloat16)
    keys, values = all_kv_ref[:, :width], all_kv_ref[:, width:]
    query, d_att = query_ref[...], datt_ref[...]
    keys_t, values_t, d_att_t = keys.T, values.T, d_att.T
    low = lax.broadcasted_iota(jnp.int32, (own, LANES), 1) < HEAD_SIZE
    none = jnp.zeros((own, LANES), jnp.bfloat16)

    for pair in range(width // LANES):
        lanes = slice(pair * LANES, (pair + 1) * LANES)
        heads = [slice(pair * LANES + h * HEAD_SIZE, pair * LANES + (h + 1) * HEAD_SIZE) for h in range(2)]
        k_pair, v_pair = keys[:, lanes], values[:, lanes]
        q_pair, d_pair = query[:, lanes], d_att[:, lanes]
        q_two = jnp.concatenate([jnp.where(low, q_pair, none), jnp.where(low, none, q_pair)], axis=0)
        d_two = jnp.concatenate([jnp.where(low, d_pair, none), jnp.where(low, none, d_pair)], axis=0)
        scores = DOT(k_pair, q_two, NT) + bias2
        top = jnp.max(scores, axis=0, keepdims=True)
        raised = jnp.exp(scores - top)
        prob = raised * (1.0 / jnp.sum(raised, axis=0, keepdims=True))
        prob_half = prob.astype(jnp.bfloat16)
        deltas = []
        for h, head in enumerate(heads):
            part = DOT(values_t[head], prob_half[:, h * own : (h + 1) * own], NN).astype(jnp.bfloat16)
            att_ref[head] = part
            deltas.append(
                jnp.sum(d_att_t[head].astype(jnp.float32) * part.astype(jnp.float32), axis=0, keepdims=True)
            )
        delta = jnp.concatenate(deltas, axis=1)
        prob_grad = DOT(v_pair, d_two, NT)
        score_grad = (prob * (prob_grad - delta)).astype(jnp.bfloat16)
        all_dkv_ref[:, lanes] = DOT(score_grad, q_two, NN).astype(jnp.bfloat16)
        all_dkv_ref[:, width + pair * LANES : width + (pair + 1) * LANES] = DOT(prob_half, d_two, NN).astype(jnp.bfloat16)
        for h, head in enumerate(heads):
            part = DOT(keys_t[head], score_grad[:, h * own : (h + 1) * own], NN) * SCALE
            dq_ref[head] = part.astype(jnp.bfloat16)
    back_ref[...] = DOT(all_dkv_ref[own:], wkv_ref[...], NT)
    dkv_ref[...] = all_dkv_ref[:own]


def final_kernel(
    rows, mask_ref, tokens_ref, grad_ref, att_ref, dq_ref, dkv_ref, wqkv_ref, wout_ref, mixed_ref, own_ref
):
    width = NH * HEAD_SIZE
    flag = token_flags(rows, mask_ref, width)
    attended = (att_ref[...].T.astype(jnp.float32) * flag).astype(jnp.bfloat16)
    mixed = tokens_ref[...].astype(jnp.float32) + DOT(attended, wout_ref[...], NN)
    mixed_ref[...] = mixed.astype(jnp.bfloat16)
    own_ref[...] = (
        grad_ref[...].astype(jnp.float32)
        + DOT(dq_ref[...].T, wqkv_ref[:, :width], NT)
        + DOT(dkv_ref[...], wqkv_ref[:, width:], NT)
    )


def call(kernel, name, outs, scratch, flops, smem, *operands):
    vmem = pl.BlockSpec(memory_space=pltpu.VMEM)
    in_specs = [pl.BlockSpec(memory_space=pltpu.SMEM)] * smem + [vmem] * (len(operands) - smem)
    moved = sum(a.size * a.dtype.itemsize for a in operands)
    return pl.pallas_call(
        kernel,
        out_shape=tuple(jax.ShapeDtypeStruct(shape, dtype) for shape, dtype in outs),
        in_specs=in_specs,
        out_specs=tuple(vmem for _ in outs),
        scratch_shapes=[pltpu.VMEM(shape, dtype) for shape, dtype in scratch],
        compiler_params=pltpu.CompilerParams(vmem_limit_bytes=40 << 20),
        cost_estimate=pl.CostEstimate(flops=flops, transcendentals=0, bytes_accessed=moved),
        name=name,
    )(*operands)


def local(tokens, w_qkv, w_out, block_mask, grad_out):
    tile_rows, tile_cols, width = tokens.shape
    count_y, count_x = lax.axis_size("gy"), lax.axis_size("gx")
    blocks = block_mask.shape[0] * block_mask.shape[1]
    rows = Rows(tile_rows, tile_cols, blocks * (count_y + count_x))
    own, side, edge, wide = rows.own, rows.side, rows.edge, rows.wide
    even_y, even_x = lax.axis_index("gy") % 2 == 0, lax.axis_index("gx") % 2 == 0
    flat_tokens = tokens.reshape(own, width)
    grad_flat = grad_out.reshape(own, width)
    half, full = jnp.bfloat16, jnp.float32

    first = tokens[:, :REACH].reshape(side, width)
    last = tokens[:, tile_cols - REACH :].reshape(side, width)
    odd_x = lax.ppermute(jnp.where(even_x, first, last), "gx", pairs_odd(count_x, False))
    grouped = tokens.astype(full).reshape(
        tile_rows // TISSUE_BLOCK, TISSUE_BLOCK, tile_cols // TISSUE_BLOCK, TISSUE_BLOCK, width
    )
    sums = (jnp.sum(grouped, axis=(1, 3)) / TISSUE_BLOCK).reshape(blocks, width).astype(half)
    marks = jnp.broadcast_to(block_mask.reshape(blocks, 1), (blocks, width)).astype(half)
    mine = jnp.concatenate([sums, marks], axis=0)
    low_x = lax.ppermute(
        jnp.concatenate([jnp.where(even_x, last, first), mine], axis=0), "gx", pairs_low(count_x)
    )
    row_pool = jnp.concatenate([mine, low_x[side:]], axis=0)
    for step in steps_above(count_x, 2):
        row_pool = jnp.concatenate([row_pool, lax.ppermute(row_pool, "gx", pairs_far(count_x, step))], axis=0)
    spread = jnp.concatenate(
        [low_x[:side].reshape(tile_rows, REACH, width), tokens, odd_x.reshape(tile_rows, REACH, width)], axis=1
    )
    top, bottom = spread[:REACH].reshape(edge, width), spread[tile_rows - REACH :].reshape(edge, width)
    low_y = lax.ppermute(
        jnp.concatenate([jnp.where(even_y, bottom, top), mine], axis=0), "gy", pairs_low(count_y)
    )
    odd_y = lax.ppermute(
        jnp.concatenate([jnp.where(even_y, top, bottom), mine, low_y[edge:]], axis=0), "gy", pairs_odd(count_y, True)
    )
    col_pool = jnp.concatenate([mine, low_y[edge:], odd_y[edge:]], axis=0)
    for step in steps_above(count_y // 2, 2):
        col_pool = jnp.concatenate([col_pool, lax.ppermute(col_pool, "gy", window_pairs(count_y, step))], axis=0)
    pool = jnp.concatenate([row_pool, col_pool], axis=0).reshape(count_x + count_y, 2, blocks, width)
    spare = ((0, rows.total - rows.used), (0, 0))
    pool_tokens = jnp.pad(pool[:, 0].reshape(-1, width), spare)
    flags = jnp.pad(pool[:, 1, :, :own].reshape(-1, own), spare).astype(full)

    macs = own * width * width
    query, kv, d_att = call(
        functools.partial(own_kernel, rows), "own", [((own, width), half), ((own, 2 * width), half), ((own, width), half)],
        [], 8 * macs, 1, block_mask, flat_tokens, grad_flat, w_qkv, w_out,
    )
    bias = window_bias(rows, count_y, count_x)
    back, d_kv, att, d_query = call(
        functools.partial(attention_kernel, rows), "attention",
        [((rows.total - own, width), full), ((own, 2 * width), half), ((width, own), half), ((width, own), half)],
        [((rows.total - own, width), half), ((rows.total, 2 * width), half), ((rows.total, 2 * width), half)],
        40 * macs, 0, low_x, odd_x, low_y, odd_y, pool_tokens, flags, bias, query, kv, d_att, w_qkv[:, width:],
    )
    mixed, own_back = call(
        functools.partial(final_kernel, rows), "final", [((own, width), half), ((own, width), full)],
        [], 8 * macs, 1, block_mask, flat_tokens, grad_flat, att, d_query, d_kv, w_qkv, w_out,
    )

    def piece(start, count):
        return back[start - own : start - own + count]

    row_grad = piece(rows.pool, count_x * blocks).reshape(count_x // 2, 2, blocks, width)
    col_grad = piece(rows.pool + count_x * blocks, count_y * blocks)
    low_edge, odd_edge = (
        piece(start, edge).reshape(REACH, wide, width) for start in (rows.low_y, rows.odd_y)
    )

    def tall(start, cols):
        return jnp.concatenate(
            [low_edge[:, cols], piece(start, side).reshape(tile_rows, REACH, width), odd_edge[:, cols]], axis=0
        ).reshape(-1, width)

    tall_rows = tile_rows + 2 * REACH
    odd_got = lax.ppermute(
        tall(rows.odd_x, slice(wide - REACH, wide)).astype(half), "gx", pairs_odd(count_x, False)
    ).astype(full).reshape(tall_rows, REACH, width)
    low_got = lax.ppermute(
        jnp.concatenate([tall(rows.low_x, slice(0, REACH)), row_grad[:, 1].reshape(-1, width)], axis=0).astype(half),
        "gx",
        pairs_low(count_x),
    ).astype(full)
    row_grad = row_grad[:, 0].reshape(-1, width) + low_got[tall_rows * REACH :]
    low_got = low_got[: tall_rows * REACH].reshape(tall_rows, REACH, width)
    for step in reversed(steps_above(count_x, 2)):
        middle = row_grad.shape[0] // 2
        row_grad = row_grad[:middle] + lax.ppermute(
            row_grad[middle:].astype(half), "gx", pairs_far(count_x, step)
        ).astype(full)
    at_first = jnp.where(even_x, odd_got, low_got)
    at_last = jnp.where(even_x, low_got, odd_got)
    room = tile_cols - REACH
    added = jnp.pad(at_first, ((0, 0), (0, room), (0, 0))) + jnp.pad(at_last, ((0, 0), (room, 0), (0, 0)))
    inner = slice(REACH, REACH + tile_cols)
    low_send = (low_edge[:, inner] + added[:REACH]).reshape(-1, width)
    odd_send = (odd_edge[:, inner] + added[tall_rows - REACH :]).reshape(-1, width)
    for step in reversed(steps_above(count_y // 2, 2)):
        middle = col_grad.shape[0] // 2
        col_grad = col_grad[:middle] + lax.ppermute(
            col_grad[middle:].astype(half), "gy", window_pairs(count_y, step)
        ).astype(full)
    strip = REACH * tile_cols
    got = lax.ppermute(
        jnp.concatenate([odd_send, col_grad[2 * blocks :]], axis=0).astype(half), "gy", pairs_odd(count_y, True)
    ).astype(full)
    odd_rows = got[:strip].reshape(REACH, tile_cols, width)
    col_grad = col_grad[: 2 * blocks] + got[strip:]
    got = lax.ppermute(
        jnp.concatenate([low_send, col_grad[blocks:]], axis=0).astype(half), "gy", pairs_low(count_y)
    ).astype(full)
    low_rows = got[:strip].reshape(REACH, tile_cols, width)
    block_grad = col_grad[:blocks] + got[strip:] + row_grad
    at_top = jnp.where(even_y, odd_rows, low_rows)
    at_bottom = jnp.where(even_y, low_rows, odd_rows)
    room = tile_rows - REACH
    d_tokens = own_back.reshape(tile_rows, tile_cols, width) + added[REACH : REACH + tile_rows]
    d_tokens = d_tokens + jnp.pad(at_top, ((0, room), (0, 0), (0, 0))) + jnp.pad(at_bottom, ((room, 0), (0, 0), (0, 0)))
    shaped = (block_grad / TISSUE_BLOCK).reshape(tile_rows // TISSUE_BLOCK, tile_cols // TISSUE_BLOCK, width)
    d_tokens = d_tokens + jnp.repeat(jnp.repeat(shaped, TISSUE_BLOCK, 0), TISSUE_BLOCK, 1)
    return mixed.reshape(tile_rows, tile_cols, width), d_tokens.astype(half)


def solution(mesh):
    placed = (P("gy", "gx", None), P(), P(), P("gy", "gx"), P("gy", "gx", None))
    return jax.shard_map(
        local,
        mesh=mesh,
        in_specs=placed,
        out_specs=(P("gy", "gx", None), P("gy", "gx", None)),
        check_vma=False,
    )
```

```python
import functools

import jax
import jax.numpy as jnp
import numpy as np
from jax import lax
from jax.experimental import pallas as pl
from jax.experimental.pallas import tpu as pltpu
from jax.sharding import PartitionSpec as P

NH = 6
HEAD_SIZE = 64
KS = 7
TISSUE_BLOCK = 8
REACH = KS // 2
NEG_FILL = -1e30
LANES = 128
ALIGN = 16
FAR = -1000


def pairs_low(count):
    return [(i, i ^ 1) for i in range(count)]


def pairs_odd(count, wrap):
    moves = []
    for i in range(count):
        j = (i + 1) % count if i % 2 else (i - 1) % count
        if wrap or abs(i - j) == 1:
            moves.append((i, j))
    return moves


def pairs_far(count, step):
    return [(i, i ^ step) for i in range(count)]


def window_pairs(count, step):
    moves = []
    for i in range(count):
        group, side = divmod((i - 1) % count, 2)
        moves.append((i, (2 * (group ^ step) + 1 + side) % count))
    return moves


def steps_above(count, first):
    steps = []
    while first < count:
        steps.append(first)
        first *= 2
    return steps


def padded(count, unit=ALIGN):
    return -(-count // unit) * unit


class Rows:
    def __init__(self, tile_rows, tile_cols, pooled):
        self.tile_rows, self.tile_cols = tile_rows, tile_cols
        self.wide = tile_cols + 2 * REACH
        self.own = tile_rows * tile_cols
        self.side = tile_rows * REACH
        self.edge = REACH * self.wide
        self.low_x = self.own
        self.odd_x = self.low_x + padded(self.side)
        self.low_y = self.odd_x + padded(self.side)
        self.odd_y = self.low_y + padded(self.edge)
        self.pool = self.odd_y + padded(self.edge)
        self.pooled = pooled
        self.used = self.pool + pooled
        self.total = padded(self.used, LANES)


def places(rows):
    tile_rows, tile_cols = rows.tile_rows, rows.tile_cols
    place = np.full((2, 2, rows.total, 2), FAR, np.int32)

    def grid(first, second):
        return np.stack(np.meshgrid(np.asarray(first), np.asarray(second), indexing="ij"), -1).reshape(-1, 2)

    before, own_cols, after = np.arange(-REACH, 0), np.arange(tile_cols), tile_cols + np.arange(REACH)
    above, own_rows, below = np.arange(-REACH, 0), np.arange(tile_rows), tile_rows + np.arange(REACH)
    for odd_y in range(2):
        for odd_x in range(2):
            low_cols, odd_cols = (before, after) if odd_x else (after, before)
            low_rows, odd_rows = (above, below) if odd_y else (below, above)
            wide_cols = np.concatenate([low_cols, own_cols, odd_cols])
            spot = place[odd_y, odd_x]
            spot[: rows.own] = grid(own_rows, own_cols)
            spot[rows.low_x : rows.low_x + rows.side] = grid(own_rows, low_cols)
            spot[rows.odd_x : rows.odd_x + rows.side] = grid(own_rows, odd_cols)
            spot[rows.low_y : rows.low_y + rows.edge] = grid(low_rows, wide_cols)
            spot[rows.odd_y : rows.odd_y + rows.edge] = grid(odd_rows, wide_cols)
    return place


def window_bias(rows, count_y, count_x):
    iy, ix = lax.axis_index("gy"), lax.axis_index("gx")
    table = jnp.asarray(places(rows))
    key = table[iy % 2, ix % 2]
    key_row, key_col = key[:, :1], key[:, 1:]
    token = np.arange(rows.own)[None, :]
    near = (jnp.abs(key_row - token // rows.tile_cols) <= REACH) & (jnp.abs(key_col - token % rows.tile_cols) <= REACH)
    row, col = iy * rows.tile_rows + key_row, ix * rows.tile_cols + key_col
    inside = (row >= 0) & (row < count_y * rows.tile_rows) & (col >= 0) & (col < count_x * rows.tile_cols)
    return jnp.where(near & inside, 0.0, NEG_FILL).astype(jnp.float32)


DOT = functools.partial(lax.dot_general, preferred_element_type=jnp.float32)
NN = (((1,), (0,)), ((), ()))
NT = (((1,), (1,)), ((), ()))
SCALE = HEAD_SIZE**-0.5


def token_flags(rows, mask_ref, width):
    token = lax.broadcasted_iota(jnp.int32, (rows.own, width), 0)
    block_cols = rows.tile_cols // TISSUE_BLOCK
    block = token // (rows.tile_cols * TISSUE_BLOCK) * block_cols + token % rows.tile_cols // TISSUE_BLOCK
    flag = jnp.zeros((rows.own, width), jnp.float32)
    for b in range(mask_ref.shape[0] * mask_ref.shape[1]):
        value = mask_ref[b // block_cols, b % block_cols].astype(jnp.float32)
        flag = jnp.where(block == b, value, flag)
    return flag


def own_kernel(rows, mask_ref, tokens_ref, grad_ref, wqkv_ref, wout_ref, query_ref, kv_ref, datt_ref):
    width = NH * HEAD_SIZE
    tokens = tokens_ref[...]
    query = DOT(tokens, wqkv_ref[:, :width], NN).astype(jnp.bfloat16).astype(jnp.float32) * SCALE
    query_ref[...] = query.astype(jnp.bfloat16)
    kv_ref[...] = DOT(tokens, wqkv_ref[:, width:], NN).astype(jnp.bfloat16)
    flag = token_flags(rows, mask_ref, width)
    datt_ref[...] = (DOT(grad_ref[...], wout_ref[...], NT) * flag).astype(jnp.bfloat16)


def attention_kernel(
    rows,
    low_x_ref, odd_x_ref, low_y_ref, odd_y_ref, pool_ref, flags_ref, bias_ref, query_ref, kv_ref, datt_ref, wkv_ref,
    back_ref, dkv_ref, att_ref, dq_ref,
    x_ref, all_kv_ref, all_dkv_ref,
):
    width = NH * HEAD_SIZE
    own = rows.own
    pooled = jnp.where(flags_ref[...] > 0, 0.0, NEG_FILL)
    bias = jnp.concatenate([bias_ref[: rows.pool], pooled], axis=0)
    bias2 = jnp.concatenate([bias, bias], axis=1)

    x_ref[...] = jnp.zeros_like(x_ref)
    for start, ref, count in (
        (rows.low_x, low_x_ref, rows.side),
        (rows.odd_x, odd_x_ref, rows.side),
        (rows.low_y, low_y_ref, rows.edge),
        (rows.odd_y, odd_y_ref, rows.edge),
        (rows.pool, pool_ref, rows.total - rows.pool),
    ):
        x_ref[start - own : start - own + count] = ref[:count]
    all_kv_ref[:own] = kv_ref[...]
    all_kv_ref[own:] = DOT(x_ref[...], wkv_ref[...], NN).astype(jnp.bfloat16)
    keys, values = all_kv_ref[:, :width], all_kv_ref[:, width:]
    query, d_att = query_ref[...], datt_ref[...]
    keys_t, values_t, d_att_t = keys.T, values.T, d_att.T
    low = lax.broadcasted_iota(jnp.int32, (own, LANES), 1) < HEAD_SIZE
    none = jnp.zeros((own, LANES), jnp.bfloat16)

    for pair in range(width // LANES):
        lanes = slice(pair * LANES, (pair + 1) * LANES)
        heads = [slice(pair * LANES + h * HEAD_SIZE, pair * LANES + (h + 1) * HEAD_SIZE) for h in range(2)]
        k_pair, v_pair = keys[:, lanes], values[:, lanes]
        q_pair, d_pair = query[:, lanes], d_att[:, lanes]
        q_two = jnp.concatenate([jnp.where(low, q_pair, none), jnp.where(low, none, q_pair)], axis=0)
        d_two = jnp.concatenate([jnp.where(low, d_pair, none), jnp.where(low, none, d_pair)], axis=0)
        scores = DOT(k_pair, q_two, NT) + bias2
        top = jnp.max(scores, axis=0, keepdims=True)
        raised = jnp.exp(scores - top)
        prob = raised * (1.0 / jnp.sum(raised, axis=0, keepdims=True))
        prob_half = prob.astype(jnp.bfloat16)
        deltas = []
        for h, head in enumerate(heads):
            part = DOT(values_t[head], prob_half[:, h * own : (h + 1) * own], NN).astype(jnp.bfloat16)
            att_ref[head] = part
            deltas.append(
                jnp.sum(d_att_t[head].astype(jnp.float32) * part.astype(jnp.float32), axis=0, keepdims=True)
            )
        delta = jnp.concatenate(deltas, axis=1)
        prob_grad = DOT(v_pair, d_two, NT)
        score_grad = (prob * (prob_grad - delta)).astype(jnp.bfloat16)
        all_dkv_ref[:, lanes] = DOT(score_grad, q_two, NN).astype(jnp.bfloat16)
        all_dkv_ref[:, width + pair * LANES : width + (pair + 1) * LANES] = DOT(prob_half, d_two, NN).astype(jnp.bfloat16)
        for h, head in enumerate(heads):
            part = DOT(keys_t[head], score_grad[:, h * own : (h + 1) * own], NN) * SCALE
            dq_ref[head] = part.astype(jnp.bfloat16)
    back_ref[...] = DOT(all_dkv_ref[own:], wkv_ref[...], NT).astype(jnp.bfloat16)
    dkv_ref[...] = all_dkv_ref[:own]


def final_kernel(
    rows, mask_ref, tokens_ref, grad_ref, att_ref, dq_ref, dkv_ref, wqkv_ref, wout_ref, mixed_ref, own_ref
):
    width = NH * HEAD_SIZE
    flag = token_flags(rows, mask_ref, width)
    attended = (att_ref[...].T.astype(jnp.float32) * flag).astype(jnp.bfloat16)
    mixed = tokens_ref[...].astype(jnp.float32) + DOT(attended, wout_ref[...], NN)
    mixed_ref[...] = mixed.astype(jnp.bfloat16)
    own_ref[...] = (
        grad_ref[...].astype(jnp.float32)
        + DOT(dq_ref[...].T, wqkv_ref[:, :width], NT)
        + DOT(dkv_ref[...], wqkv_ref[:, width:], NT)
    )


def call(kernel, name, outs, scratch, flops, smem, *operands):
    vmem = pl.BlockSpec(memory_space=pltpu.VMEM)
    in_specs = [pl.BlockSpec(memory_space=pltpu.SMEM)] * smem + [vmem] * (len(operands) - smem)
    moved = sum(a.size * a.dtype.itemsize for a in operands)
    return pl.pallas_call(
        kernel,
        out_shape=tuple(jax.ShapeDtypeStruct(shape, dtype) for shape, dtype in outs),
        in_specs=in_specs,
        out_specs=tuple(vmem for _ in outs),
        scratch_shapes=[pltpu.VMEM(shape, dtype) for shape, dtype in scratch],
        compiler_params=pltpu.CompilerParams(vmem_limit_bytes=40 << 20),
        cost_estimate=pl.CostEstimate(flops=flops, transcendentals=0, bytes_accessed=moved),
        name=name,
    )(*operands)


def swap(name, value, axis, moves):
    with jax.named_scope(name):
        return lax.ppermute(value, axis, moves)


def local(tokens, w_qkv, w_out, block_mask, grad_out):
    tile_rows, tile_cols, width = tokens.shape
    count_y, count_x = lax.axis_size("gy"), lax.axis_size("gx")
    blocks = block_mask.shape[0] * block_mask.shape[1]
    rows = Rows(tile_rows, tile_cols, blocks * (count_y + count_x))
    own, side, edge, wide = rows.own, rows.side, rows.edge, rows.wide
    even_y, even_x = lax.axis_index("gy") % 2 == 0, lax.axis_index("gx") % 2 == 0
    flat_tokens = tokens.reshape(own, width)
    grad_flat = grad_out.reshape(own, width)
    half, full = jnp.bfloat16, jnp.float32

    first = tokens[:, :REACH].reshape(side, width)
    last = tokens[:, tile_cols - REACH :].reshape(side, width)
    odd_x = swap("r1_odd_columns", jnp.where(even_x, first, last), "gx", pairs_odd(count_x, False))
    grouped = tokens.astype(full).reshape(
        tile_rows // TISSUE_BLOCK, TISSUE_BLOCK, tile_cols // TISSUE_BLOCK, TISSUE_BLOCK, width
    )
    sums = (jnp.sum(grouped, axis=(1, 3)) / TISSUE_BLOCK).reshape(blocks, width).astype(half)
    marks = jnp.broadcast_to(block_mask.reshape(blocks, 1), (blocks, width)).astype(half)
    mine = jnp.concatenate([sums, marks], axis=0)
    low_x = swap("r1_low_columns",
        jnp.concatenate([jnp.where(even_x, last, first), mine], axis=0), "gx", pairs_low(count_x)
    )
    row_pool = jnp.concatenate([mine, low_x[side:]], axis=0)
    for step in steps_above(count_x, 2):
        row_pool = jnp.concatenate([row_pool, swap(f"r1_far_columns_{step}", row_pool, "gx", pairs_far(count_x, step))], axis=0)
    spread = jnp.concatenate(
        [low_x[:side].reshape(tile_rows, REACH, width), tokens, odd_x.reshape(tile_rows, REACH, width)], axis=1
    )
    top, bottom = spread[:REACH].reshape(edge, width), spread[tile_rows - REACH :].reshape(edge, width)
    low_y = swap("r1_low_rows",
        jnp.concatenate([jnp.where(even_y, bottom, top), mine], axis=0), "gy", pairs_low(count_y)
    )
    odd_y = swap("r1_odd_rows",
        jnp.concatenate([jnp.where(even_y, top, bottom), mine, low_y[edge:]], axis=0), "gy", pairs_odd(count_y, True)
    )
    col_pool = jnp.concatenate([mine, low_y[edge:], odd_y[edge:]], axis=0)
    for step in steps_above(count_y // 2, 2):
        col_pool = jnp.concatenate([col_pool, swap(f"r1_far_rows_{step}", col_pool, "gy", window_pairs(count_y, step))], axis=0)
    pool = jnp.concatenate([row_pool, col_pool], axis=0).reshape(count_x + count_y, 2, blocks, width)
    spare = ((0, rows.total - rows.used), (0, 0))
    pool_tokens = jnp.pad(pool[:, 0].reshape(-1, width), spare)
    flags = jnp.pad(pool[:, 1, :, :own].reshape(-1, own), spare).astype(full)

    macs = own * width * width
    query, kv, d_att = call(
        functools.partial(own_kernel, rows), "own", [((own, width), half), ((own, 2 * width), half), ((own, width), half)],
        [], 8 * macs, 1, block_mask, flat_tokens, grad_flat, w_qkv, w_out,
    )
    bias = window_bias(rows, count_y, count_x)
    back, d_kv, att, d_query = call(
        functools.partial(attention_kernel, rows), "attention",
        [((rows.total - own, width), half), ((own, 2 * width), half), ((width, own), half), ((width, own), half)],
        [((rows.total - own, width), half), ((rows.total, 2 * width), half), ((rows.total, 2 * width), half)],
        40 * macs, 0, low_x, odd_x, low_y, odd_y, pool_tokens, flags, bias, query, kv, d_att, w_qkv[:, width:],
    )
    mixed, own_back = call(
        functools.partial(final_kernel, rows), "final", [((own, width), half), ((own, width), full)],
        [], 8 * macs, 1, block_mask, flat_tokens, grad_flat, att, d_query, d_kv, w_qkv, w_out,
    )

    def piece(start, count):
        return back[start - own : start - own + count]

    def fold(grads, got):
        return (grads.astype(full) + got.astype(full)).astype(half)

    row_grad = piece(rows.pool, count_x * blocks)
    col_grad = piece(rows.pool + count_x * blocks, count_y * blocks)
    for step in reversed(steps_above(count_x, 2)):
        if step == 2:
            row_grad, own_back = lax.optimization_barrier((row_grad, own_back))
        middle = row_grad.shape[0] // 2
        got = swap(f"r2_far_columns_{step}", row_grad[middle:], "gx", pairs_far(count_x, step))
        row_grad = fold(row_grad[:middle], got)
    for step in reversed(steps_above(count_y // 2, 2)):
        middle = col_grad.shape[0] // 2
        got = swap(f"r2_far_rows_{step}", col_grad[middle:], "gy", window_pairs(count_y, step))
        col_grad = fold(col_grad[:middle], got)
    odd_rows = swap(
        "r2_odd_rows",
        jnp.concatenate([piece(rows.odd_y, edge), col_grad[2 * blocks :]], axis=0),
        "gy",
        pairs_odd(count_y, True),
    )
    col_grad = fold(col_grad[: 2 * blocks], odd_rows[edge:])
    low_rows = swap(
        "r2_low_rows", jnp.concatenate([piece(rows.low_y, edge), col_grad[blocks:]], axis=0), "gy", pairs_low(count_y)
    )
    col_grad = fold(col_grad[:blocks], low_rows[edge:])
    odd_rows = odd_rows[:edge].astype(full).reshape(REACH, wide, width)
    low_rows = low_rows[:edge].astype(full).reshape(REACH, wide, width)
    at_top, at_bottom = jnp.where(even_y, odd_rows, low_rows), jnp.where(even_y, low_rows, odd_rows)
    room = tile_rows - REACH

    def lines(start, stop):
        top, bottom = at_top[:, start:stop], at_bottom[:, start:stop]
        return jnp.pad(top, ((0, room), (0, 0), (0, 0))) + jnp.pad(bottom, ((room, 0), (0, 0), (0, 0)))

    odd_side = piece(rows.odd_x, side).astype(full) + lines(wide - REACH, wide).reshape(side, width)
    odd_got = swap("r2_odd_columns", odd_side.astype(half), "gx", pairs_odd(count_x, False))
    low_side = piece(rows.low_x, side).astype(full) + lines(0, REACH).reshape(side, width)
    low_got = swap(
        "r2_low_columns",
        jnp.concatenate([low_side.astype(half), row_grad[blocks:]], axis=0),
        "gx",
        pairs_low(count_x),
    )
    block_grad = row_grad[:blocks].astype(full) + low_got[side:].astype(full) + col_grad.astype(full)
    odd_got = odd_got.astype(full).reshape(tile_rows, REACH, width)
    low_got = low_got[:side].astype(full).reshape(tile_rows, REACH, width)
    at_first, at_last = jnp.where(even_x, odd_got, low_got), jnp.where(even_x, low_got, odd_got)
    room = tile_cols - REACH
    d_tokens = own_back.reshape(tile_rows, tile_cols, width) + jnp.pad(
        at_top[:, REACH : REACH + tile_cols], ((0, tile_rows - REACH), (0, 0), (0, 0))
    )
    d_tokens = d_tokens + jnp.pad(at_bottom[:, REACH : REACH + tile_cols], ((tile_rows - REACH, 0), (0, 0), (0, 0)))
    d_tokens = d_tokens + jnp.pad(at_first, ((0, 0), (0, room), (0, 0))) + jnp.pad(at_last, ((0, 0), (room, 0), (0, 0)))
    shaped = (block_grad / TISSUE_BLOCK).reshape(tile_rows // TISSUE_BLOCK, tile_cols // TISSUE_BLOCK, width)
    d_tokens = d_tokens + jnp.repeat(jnp.repeat(shaped, TISSUE_BLOCK, 0), TISSUE_BLOCK, 1)
    return mixed.reshape(tile_rows, tile_cols, width), d_tokens.astype(half)


def solution(mesh):
    placed = (P("gy", "gx", None), P(), P(), P("gy", "gx"), P("gy", "gx", None))
    return jax.shard_map(
        local,
        mesh=mesh,
        in_specs=placed,
        out_specs=(P("gy", "gx", None), P("gy", "gx", None)),
        check_vma=False,
    )
```

```python
import functools

import jax
import jax.numpy as jnp
import numpy as np
from jax import lax
from jax.experimental import pallas as pl
from jax.experimental.pallas import tpu as pltpu
from jax.sharding import PartitionSpec as P

NH = 6
HEAD_SIZE = 64
KS = 7
TISSUE_BLOCK = 8
REACH = KS // 2
NEG_FILL = -1e30
LANES = 128
ALIGN = 16
FAR = -1000


def pairs_low(count):
    return [(i, i ^ 1) for i in range(count)]


def pairs_odd(count, wrap):
    moves = []
    for i in range(count):
        j = (i + 1) % count if i % 2 else (i - 1) % count
        if wrap or abs(i - j) == 1:
            moves.append((i, j))
    return moves


def pairs_far(count, step):
    return [(i, i ^ step) for i in range(count)]


def window_pairs(count, step):
    moves = []
    for i in range(count):
        group, side = divmod((i - 1) % count, 2)
        moves.append((i, (2 * (group ^ step) + 1 + side) % count))
    return moves


def steps_above(count, first):
    steps = []
    while first < count:
        steps.append(first)
        first *= 2
    return steps


def padded(count, unit=ALIGN):
    return -(-count // unit) * unit


class Rows:
    def __init__(self, tile_rows, tile_cols, pooled):
        self.tile_rows, self.tile_cols = tile_rows, tile_cols
        self.wide = tile_cols + 2 * REACH
        self.own = tile_rows * tile_cols
        self.side = tile_rows * REACH
        self.edge = REACH * self.wide
        self.low_x = self.own
        self.odd_x = self.low_x + padded(self.side)
        self.low_y = self.odd_x + padded(self.side)
        self.odd_y = self.low_y + padded(self.edge)
        self.pool = self.odd_y + padded(self.edge)
        self.pooled = pooled
        self.used = self.pool + pooled
        self.total = padded(self.used, LANES)


def places(rows):
    tile_rows, tile_cols = rows.tile_rows, rows.tile_cols
    place = np.full((2, 2, rows.total, 2), FAR, np.int32)

    def grid(first, second):
        return np.stack(np.meshgrid(np.asarray(first), np.asarray(second), indexing="ij"), -1).reshape(-1, 2)

    before, own_cols, after = np.arange(-REACH, 0), np.arange(tile_cols), tile_cols + np.arange(REACH)
    above, own_rows, below = np.arange(-REACH, 0), np.arange(tile_rows), tile_rows + np.arange(REACH)
    for odd_y in range(2):
        for odd_x in range(2):
            low_cols, odd_cols = (before, after) if odd_x else (after, before)
            low_rows, odd_rows = (above, below) if odd_y else (below, above)
            wide_cols = np.concatenate([low_cols, own_cols, odd_cols])
            spot = place[odd_y, odd_x]
            spot[: rows.own] = grid(own_rows, own_cols)
            spot[rows.low_x : rows.low_x + rows.side] = grid(own_rows, low_cols)
            spot[rows.odd_x : rows.odd_x + rows.side] = grid(own_rows, odd_cols)
            spot[rows.low_y : rows.low_y + rows.edge] = grid(low_rows, wide_cols)
            spot[rows.odd_y : rows.odd_y + rows.edge] = grid(odd_rows, wide_cols)
    return place


def window_bias(rows, count_y, count_x):
    iy, ix = lax.axis_index("gy"), lax.axis_index("gx")
    table = jnp.asarray(places(rows))
    key = table[iy % 2, ix % 2]
    key_row, key_col = key[:, :1], key[:, 1:]
    token = np.arange(rows.own)[None, :]
    near = (jnp.abs(key_row - token // rows.tile_cols) <= REACH) & (jnp.abs(key_col - token % rows.tile_cols) <= REACH)
    row, col = iy * rows.tile_rows + key_row, ix * rows.tile_cols + key_col
    inside = (row >= 0) & (row < count_y * rows.tile_rows) & (col >= 0) & (col < count_x * rows.tile_cols)
    return jnp.where(near & inside, 0.0, NEG_FILL).astype(jnp.float32)


DOT = functools.partial(lax.dot_general, preferred_element_type=jnp.float32)
NN = (((1,), (0,)), ((), ()))
NT = (((1,), (1,)), ((), ()))
SCALE = HEAD_SIZE**-0.5


def token_flags(rows, mask_ref, width):
    token = lax.broadcasted_iota(jnp.int32, (rows.own, width), 0)
    block_cols = rows.tile_cols // TISSUE_BLOCK
    block = token // (rows.tile_cols * TISSUE_BLOCK) * block_cols + token % rows.tile_cols // TISSUE_BLOCK
    flag = jnp.zeros((rows.own, width), jnp.float32)
    for b in range(mask_ref.shape[0] * mask_ref.shape[1]):
        value = mask_ref[b // block_cols, b % block_cols].astype(jnp.float32)
        flag = jnp.where(block == b, value, flag)
    return flag


def own_kernel(rows, mask_ref, tokens_ref, grad_ref, wqkv_ref, wout_ref, query_ref, kv_ref, datt_ref):
    width = NH * HEAD_SIZE
    tokens = tokens_ref[...]
    query = DOT(tokens, wqkv_ref[:, :width], NN).astype(jnp.bfloat16).astype(jnp.float32) * SCALE
    query_ref[...] = query.astype(jnp.bfloat16)
    kv_ref[...] = DOT(tokens, wqkv_ref[:, width:], NN).astype(jnp.bfloat16)
    flag = token_flags(rows, mask_ref, width)
    datt_ref[...] = (DOT(grad_ref[...], wout_ref[...], NT) * flag).astype(jnp.bfloat16)


def attention_kernel(
    rows,
    low_x_ref, odd_x_ref, low_y_ref, odd_y_ref, pool_ref, flags_ref, bias_ref, query_ref, kv_ref, datt_ref, wkv_ref,
    back_ref, dkv_ref, att_ref, dq_ref,
    x_ref, all_kv_ref, all_dkv_ref,
):
    width = NH * HEAD_SIZE
    own = rows.own
    pooled = jnp.where(flags_ref[...] > 0, 0.0, NEG_FILL)
    bias = jnp.concatenate([bias_ref[: rows.pool], pooled], axis=0)
    bias2 = jnp.concatenate([bias, bias], axis=1)

    x_ref[...] = jnp.zeros_like(x_ref)
    for start, ref, count in (
        (rows.low_x, low_x_ref, rows.side),
        (rows.odd_x, odd_x_ref, rows.side),
        (rows.low_y, low_y_ref, rows.edge),
        (rows.odd_y, odd_y_ref, rows.edge),
        (rows.pool, pool_ref, rows.total - rows.pool),
    ):
        x_ref[start - own : start - own + count] = ref[:count]
    all_kv_ref[:own] = kv_ref[...]
    all_kv_ref[own:] = DOT(x_ref[...], wkv_ref[...], NN).astype(jnp.bfloat16)
    keys, values = all_kv_ref[:, :width], all_kv_ref[:, width:]
    query, d_att = query_ref[...], datt_ref[...]
    keys_t, values_t, d_att_t = keys.T, values.T, d_att.T
    low = lax.broadcasted_iota(jnp.int32, (own, LANES), 1) < HEAD_SIZE
    none = jnp.zeros((own, LANES), jnp.bfloat16)

    for pair in range(width // LANES):
        lanes = slice(pair * LANES, (pair + 1) * LANES)
        heads = [slice(pair * LANES + h * HEAD_SIZE, pair * LANES + (h + 1) * HEAD_SIZE) for h in range(2)]
        k_pair, v_pair = keys[:, lanes], values[:, lanes]
        q_pair, d_pair = query[:, lanes], d_att[:, lanes]
        q_two = jnp.concatenate([jnp.where(low, q_pair, none), jnp.where(low, none, q_pair)], axis=0)
        d_two = jnp.concatenate([jnp.where(low, d_pair, none), jnp.where(low, none, d_pair)], axis=0)
        scores = DOT(k_pair, q_two, NT) + bias2
        top = jnp.max(scores, axis=0, keepdims=True)
        raised = jnp.exp(scores - top)
        prob = raised * (1.0 / jnp.sum(raised, axis=0, keepdims=True))
        prob_half = prob.astype(jnp.bfloat16)
        deltas = []
        for h, head in enumerate(heads):
            part = DOT(values_t[head], prob_half[:, h * own : (h + 1) * own], NN).astype(jnp.bfloat16)
            att_ref[head] = part
            deltas.append(
                jnp.sum(d_att_t[head].astype(jnp.float32) * part.astype(jnp.float32), axis=0, keepdims=True)
            )
        delta = jnp.concatenate(deltas, axis=1)
        prob_grad = DOT(v_pair, d_two, NT)
        score_grad = (prob * (prob_grad - delta)).astype(jnp.bfloat16)
        all_dkv_ref[:, lanes] = DOT(score_grad, q_two, NN).astype(jnp.bfloat16)
        all_dkv_ref[:, width + pair * LANES : width + (pair + 1) * LANES] = DOT(prob_half, d_two, NN).astype(jnp.bfloat16)
        for h, head in enumerate(heads):
            part = DOT(keys_t[head], score_grad[:, h * own : (h + 1) * own], NN) * SCALE
            dq_ref[head] = part.astype(jnp.bfloat16)
    back_ref[...] = DOT(all_dkv_ref[own:], wkv_ref[...], NT).astype(jnp.bfloat16)
    dkv_ref[...] = all_dkv_ref[:own]


def final_kernel(
    rows, mask_ref, tokens_ref, grad_ref, att_ref, dq_ref, dkv_ref, wqkv_ref, wout_ref, mixed_ref, own_ref
):
    width = NH * HEAD_SIZE
    flag = token_flags(rows, mask_ref, width)
    attended = (att_ref[...].T.astype(jnp.float32) * flag).astype(jnp.bfloat16)
    mixed = tokens_ref[...].astype(jnp.float32) + DOT(attended, wout_ref[...], NN)
    mixed_ref[...] = mixed.astype(jnp.bfloat16)
    own_ref[...] = (
        grad_ref[...].astype(jnp.float32)
        + DOT(dq_ref[...].T, wqkv_ref[:, :width], NT)
        + DOT(dkv_ref[...], wqkv_ref[:, width:], NT)
    )


def call(kernel, name, outs, scratch, flops, smem, *operands):
    vmem = pl.BlockSpec(memory_space=pltpu.VMEM)
    in_specs = [pl.BlockSpec(memory_space=pltpu.SMEM)] * smem + [vmem] * (len(operands) - smem)
    moved = sum(a.size * a.dtype.itemsize for a in operands)
    return pl.pallas_call(
        kernel,
        out_shape=tuple(jax.ShapeDtypeStruct(shape, dtype) for shape, dtype in outs),
        in_specs=in_specs,
        out_specs=tuple(vmem for _ in outs),
        scratch_shapes=[pltpu.VMEM(shape, dtype) for shape, dtype in scratch],
        compiler_params=pltpu.CompilerParams(vmem_limit_bytes=40 << 20),
        cost_estimate=pl.CostEstimate(flops=flops, transcendentals=0, bytes_accessed=moved),
        name=name,
    )(*operands)


def swap(name, value, axis, moves):
    with jax.named_scope(name):
        return lax.ppermute(value, axis, moves)


def local(tokens, w_qkv, w_out, block_mask, grad_out):
    tile_rows, tile_cols, width = tokens.shape
    count_y, count_x = lax.axis_size("gy"), lax.axis_size("gx")
    blocks = block_mask.shape[0] * block_mask.shape[1]
    rows = Rows(tile_rows, tile_cols, blocks * (count_y + count_x))
    own, side, edge, wide = rows.own, rows.side, rows.edge, rows.wide
    even_y, even_x = lax.axis_index("gy") % 2 == 0, lax.axis_index("gx") % 2 == 0
    flat_tokens = tokens.reshape(own, width)
    grad_flat = grad_out.reshape(own, width)
    half, full = jnp.bfloat16, jnp.float32

    first = tokens[:, :REACH].reshape(side, width)
    last = tokens[:, tile_cols - REACH :].reshape(side, width)
    odd_send = jnp.where(even_x, first, last)
    odd_x = swap("r1_odd_columns", odd_send, "gx", pairs_odd(count_x, False))
    tokens_later, _ = lax.optimization_barrier((tokens, odd_send))
    grouped = tokens_later.astype(full).reshape(
        tile_rows // TISSUE_BLOCK, TISSUE_BLOCK, tile_cols // TISSUE_BLOCK, TISSUE_BLOCK, width
    )
    sums = (jnp.sum(grouped, axis=(1, 3)) / TISSUE_BLOCK).reshape(blocks, width).astype(half)
    marks = jnp.broadcast_to(block_mask.reshape(blocks, 1), (blocks, width)).astype(half)
    mine = jnp.concatenate([sums, marks], axis=0)
    low_x = swap("r1_low_columns",
        jnp.concatenate([jnp.where(even_x, last, first), mine], axis=0), "gx", pairs_low(count_x)
    )
    row_pool = jnp.concatenate([mine, low_x[side:]], axis=0)
    for step in steps_above(count_x, 2):
        row_pool = jnp.concatenate([row_pool, swap(f"r1_far_columns_{step}", row_pool, "gx", pairs_far(count_x, step))], axis=0)
    spread = jnp.concatenate(
        [low_x[:side].reshape(tile_rows, REACH, width), tokens, odd_x.reshape(tile_rows, REACH, width)], axis=1
    )
    top, bottom = spread[:REACH].reshape(edge, width), spread[tile_rows - REACH :].reshape(edge, width)
    low_y = swap("r1_low_rows",
        jnp.concatenate([jnp.where(even_y, bottom, top), mine], axis=0), "gy", pairs_low(count_y)
    )
    odd_y = swap("r1_odd_rows",
        jnp.concatenate([jnp.where(even_y, top, bottom), mine, low_y[edge:]], axis=0), "gy", pairs_odd(count_y, True)
    )
    col_pool = jnp.concatenate([mine, low_y[edge:], odd_y[edge:]], axis=0)
    for step in steps_above(count_y // 2, 2):
        col_pool = jnp.concatenate([col_pool, swap(f"r1_far_rows_{step}", col_pool, "gy", window_pairs(count_y, step))], axis=0)
    pool = jnp.concatenate([row_pool, col_pool], axis=0).reshape(count_x + count_y, 2, blocks, width)
    spare = ((0, rows.total - rows.used), (0, 0))
    pool_tokens = jnp.pad(pool[:, 0].reshape(-1, width), spare)
    flags = jnp.pad(pool[:, 1, :, :own].reshape(-1, own), spare).astype(full)

    macs = own * width * width
    query, kv, d_att = call(
        functools.partial(own_kernel, rows), "own", [((own, width), half), ((own, 2 * width), half), ((own, width), half)],
        [], 8 * macs, 1, block_mask, flat_tokens, grad_flat, w_qkv, w_out,
    )
    bias = window_bias(rows, count_y, count_x)
    back, d_kv, att, d_query = call(
        functools.partial(attention_kernel, rows), "attention",
        [((rows.total - own, width), half), ((own, 2 * width), half), ((width, own), half), ((width, own), half)],
        [((rows.total - own, width), half), ((rows.total, 2 * width), half), ((rows.total, 2 * width), half)],
        40 * macs, 0, low_x, odd_x, low_y, odd_y, pool_tokens, flags, bias, query, kv, d_att, w_qkv[:, width:],
    )
    def piece(start, count):
        return back[start - own : start - own + count]

    def fold(grads, got):
        return (grads.astype(full) + got.astype(full)).astype(half)

    row_grad = piece(rows.pool, count_x * blocks)
    col_grad = piece(rows.pool + count_x * blocks, count_y * blocks)
    for step in reversed(steps_above(count_y // 2, 2)):
        middle = col_grad.shape[0] // 2
        got = swap(f"r2_far_rows_{step}", col_grad[middle:], "gy", window_pairs(count_y, step))
        col_grad = fold(col_grad[:middle], got)
    odd_rows = swap(
        "r2_odd_rows",
        jnp.concatenate([piece(rows.odd_y, edge), col_grad[2 * blocks :]], axis=0),
        "gy",
        pairs_odd(count_y, True),
    )
    col_grad = fold(col_grad[: 2 * blocks], odd_rows[edge:])
    low_rows = swap(
        "r2_low_rows", jnp.concatenate([piece(rows.low_y, edge), col_grad[blocks:]], axis=0), "gy", pairs_low(count_y)
    )
    for step in reversed(steps_above(count_x, 2)):
        if step == 2:
            row_grad, low_rows = lax.optimization_barrier((row_grad, low_rows))
        middle = row_grad.shape[0] // 2
        got = swap(f"r2_far_columns_{step}", row_grad[middle:], "gx", pairs_far(count_x, step))
        row_grad = fold(row_grad[:middle], got)
    att, row_grad = lax.optimization_barrier((att, row_grad))
    mixed, own_back = call(
        functools.partial(final_kernel, rows), "final", [((own, width), half), ((own, width), full)],
        [], 8 * macs, 1, block_mask, flat_tokens, grad_flat, att, d_query, d_kv, w_qkv, w_out,
    )
    col_grad = fold(col_grad[:blocks], low_rows[edge:])
    odd_rows = odd_rows[:edge].astype(full).reshape(REACH, wide, width)
    low_rows = low_rows[:edge].astype(full).reshape(REACH, wide, width)
    at_top, at_bottom = jnp.where(even_y, odd_rows, low_rows), jnp.where(even_y, low_rows, odd_rows)
    room = tile_rows - REACH

    def lines(start, stop):
        top, bottom = at_top[:, start:stop], at_bottom[:, start:stop]
        return jnp.pad(top, ((0, room), (0, 0), (0, 0))) + jnp.pad(bottom, ((room, 0), (0, 0), (0, 0)))

    odd_side = piece(rows.odd_x, side).astype(full) + lines(wide - REACH, wide).reshape(side, width)
    odd_got = swap("r2_odd_columns", odd_side.astype(half), "gx", pairs_odd(count_x, False))
    low_side = piece(rows.low_x, side).astype(full) + lines(0, REACH).reshape(side, width)
    room = tile_cols - REACH
    d_tokens = own_back.reshape(tile_rows, tile_cols, width) + jnp.pad(
        at_top[:, REACH : REACH + tile_cols], ((0, tile_rows - REACH), (0, 0), (0, 0))
    )
    d_tokens = d_tokens + jnp.pad(at_bottom[:, REACH : REACH + tile_cols], ((tile_rows - REACH, 0), (0, 0), (0, 0)))

    def columns(got, at_first):
        got = got.astype(full).reshape(tile_rows, REACH, width)
        first, last = jnp.pad(got, ((0, 0), (0, room), (0, 0))), jnp.pad(got, ((0, 0), (room, 0), (0, 0)))
        return jnp.where(at_first, first, last)

    d_tokens = d_tokens + columns(odd_got, even_x)
    low_got = swap(
        "r2_low_columns",
        jnp.concatenate([low_side.astype(half), row_grad[blocks:]], axis=0),
        "gx",
        pairs_low(count_x),
    )
    low_got, d_tokens = lax.optimization_barrier((low_got, d_tokens))
    block_grad = row_grad[:blocks].astype(full) + low_got[side:].astype(full) + col_grad.astype(full)
    d_tokens = d_tokens + columns(low_got[:side], ~even_x)
    shaped = (block_grad / TISSUE_BLOCK).reshape(tile_rows // TISSUE_BLOCK, tile_cols // TISSUE_BLOCK, width)
    d_tokens = d_tokens + jnp.repeat(jnp.repeat(shaped, TISSUE_BLOCK, 0), TISSUE_BLOCK, 1)
    return mixed.reshape(tile_rows, tile_cols, width), d_tokens.astype(half)


def solution(mesh):
    placed = (P("gy", "gx", None), P(), P(), P("gy", "gx"), P("gy", "gx", None))
    return jax.shard_map(
        local,
        mesh=mesh,
        in_specs=placed,
        out_specs=(P("gy", "gx", None), P("gy", "gx", None)),
        check_vma=False,
    )
```

```python
import functools

import jax
import jax.numpy as jnp
import numpy as np
from jax import lax
from jax.experimental import pallas as pl
from jax.experimental.pallas import tpu as pltpu
from jax.sharding import PartitionSpec as P

NH = 6
HEAD_SIZE = 64
KS = 7
TISSUE_BLOCK = 8
REACH = KS // 2
NEG_FILL = -1e30
LANES = 128
ALIGN = 16
FAR = -1000


def pairs_low(count):
    return [(i, i ^ 1) for i in range(count)]


def pairs_odd(count, wrap):
    moves = []
    for i in range(count):
        j = (i + 1) % count if i % 2 else (i - 1) % count
        if wrap or abs(i - j) == 1:
            moves.append((i, j))
    return moves


def pairs_far(count, step):
    return [(i, i ^ step) for i in range(count)]


def window_pairs(count, step):
    moves = []
    for i in range(count):
        group, side = divmod((i - 1) % count, 2)
        moves.append((i, (2 * (group ^ step) + 1 + side) % count))
    return moves


def steps_above(count, first):
    steps = []
    while first < count:
        steps.append(first)
        first *= 2
    return steps


def padded(count, unit=ALIGN):
    return -(-count // unit) * unit


class Rows:
    def __init__(self, tile_rows, tile_cols, pooled):
        self.tile_rows, self.tile_cols = tile_rows, tile_cols
        self.wide = tile_cols + 2 * REACH
        self.own = tile_rows * tile_cols
        self.side = tile_rows * REACH
        self.edge = REACH * self.wide
        self.low_x = self.own
        self.odd_x = self.low_x + padded(self.side)
        self.low_y = self.odd_x + padded(self.side)
        self.odd_y = self.low_y + padded(self.edge)
        self.pool = self.odd_y + padded(self.edge)
        self.pooled = pooled
        self.used = self.pool + pooled
        self.total = padded(self.used, LANES)


def places(rows):
    tile_rows, tile_cols = rows.tile_rows, rows.tile_cols
    place = np.full((2, 2, rows.total, 2), FAR, np.int32)

    def grid(first, second):
        return np.stack(np.meshgrid(np.asarray(first), np.asarray(second), indexing="ij"), -1).reshape(-1, 2)

    before, own_cols, after = np.arange(-REACH, 0), np.arange(tile_cols), tile_cols + np.arange(REACH)
    above, own_rows, below = np.arange(-REACH, 0), np.arange(tile_rows), tile_rows + np.arange(REACH)
    for odd_y in range(2):
        for odd_x in range(2):
            low_cols, odd_cols = (before, after) if odd_x else (after, before)
            low_rows, odd_rows = (above, below) if odd_y else (below, above)
            wide_cols = np.concatenate([low_cols, own_cols, odd_cols])
            spot = place[odd_y, odd_x]
            spot[: rows.own] = grid(own_rows, own_cols)
            spot[rows.low_x : rows.low_x + rows.side] = grid(own_rows, low_cols)
            spot[rows.odd_x : rows.odd_x + rows.side] = grid(own_rows, odd_cols)
            spot[rows.low_y : rows.low_y + rows.edge] = grid(low_rows, wide_cols)
            spot[rows.odd_y : rows.odd_y + rows.edge] = grid(odd_rows, wide_cols)
    return place


def window_bias(rows, count_y, count_x):
    iy, ix = lax.axis_index("gy"), lax.axis_index("gx")
    table = jnp.asarray(places(rows))
    key = table[iy % 2, ix % 2]
    key_row, key_col = key[:, :1], key[:, 1:]
    token = np.arange(rows.own)[None, :]
    near = (jnp.abs(key_row - token // rows.tile_cols) <= REACH) & (jnp.abs(key_col - token % rows.tile_cols) <= REACH)
    row, col = iy * rows.tile_rows + key_row, ix * rows.tile_cols + key_col
    inside = (row >= 0) & (row < count_y * rows.tile_rows) & (col >= 0) & (col < count_x * rows.tile_cols)
    return jnp.where(near & inside, 0.0, NEG_FILL).astype(jnp.float32)


DOT = functools.partial(lax.dot_general, preferred_element_type=jnp.float32)
NN = (((1,), (0,)), ((), ()))
NT = (((1,), (1,)), ((), ()))
SCALE = HEAD_SIZE**-0.5


def token_flags(rows, mask_ref, width):
    token = lax.broadcasted_iota(jnp.int32, (rows.own, width), 0)
    block_cols = rows.tile_cols // TISSUE_BLOCK
    block = token // (rows.tile_cols * TISSUE_BLOCK) * block_cols + token % rows.tile_cols // TISSUE_BLOCK
    flag = jnp.zeros((rows.own, width), jnp.float32)
    for b in range(mask_ref.shape[0] * mask_ref.shape[1]):
        value = mask_ref[b // block_cols, b % block_cols].astype(jnp.float32)
        flag = jnp.where(block == b, value, flag)
    return flag


def two_heads(pair, own, query, d_att):
    low = lax.broadcasted_iota(jnp.int32, (own, LANES), 1) < HEAD_SIZE
    none = jnp.zeros((own, LANES), jnp.bfloat16)

    def stack(field):
        part = field[:, pair * LANES : (pair + 1) * LANES]
        return jnp.concatenate([jnp.where(low, part, none), jnp.where(low, none, part)], axis=0)

    return stack(query), stack(d_att)


def window_kernel(
    rows,
    mask_ref, tokens_ref, low_x_ref, odd_x_ref, low_y_ref, odd_y_ref, bias_ref, grad_ref, wqkv_ref, wout_ref,
    query_ref, datt_ref, datt_t_ref, kv_t_ref, raised_ref, stats_ref, grads_ref,
    x_ref,
):
    width = NH * HEAD_SIZE
    own, count = rows.own, rows.pool
    tokens = tokens_ref[...]
    x_ref[...] = jnp.zeros_like(x_ref)
    x_ref[:own] = tokens
    for start, ref, size in (
        (rows.low_x, low_x_ref, rows.side),
        (rows.odd_x, odd_x_ref, rows.side),
        (rows.low_y, low_y_ref, rows.edge),
        (rows.odd_y, odd_y_ref, rows.edge),
    ):
        x_ref[start : start + size] = ref[:size]
    query = DOT(tokens, wqkv_ref[:, :width], NN).astype(jnp.bfloat16).astype(jnp.float32) * SCALE
    query = query.astype(jnp.bfloat16)
    query_ref[...] = query
    flag = token_flags(rows, mask_ref, width)
    d_att = (DOT(grad_ref[...], wout_ref[...], NT) * flag).astype(jnp.bfloat16)
    datt_ref[...] = d_att
    datt_t_ref[...] = d_att.T
    kv = DOT(x_ref[...], wqkv_ref[:, width:], NN).astype(jnp.bfloat16)
    kv_t_ref[...] = kv.T
    bias = bias_ref[:count]
    bias2 = jnp.concatenate([bias, bias], axis=1)
    tops, totals = [], []
    for pair in range(width // LANES):
        lanes = slice(pair * LANES, (pair + 1) * LANES)
        q_two, d_two = two_heads(pair, own, query, d_att)
        scores = DOT(kv[:, lanes], q_two, NT) + bias2
        top = jnp.max(scores, axis=0, keepdims=True)
        raised = jnp.exp(scores - top)
        raised_ref[pair * count : (pair + 1) * count] = raised
        grads_ref[pair * count : (pair + 1) * count] = DOT(kv[:, width + pair * LANES : width + (pair + 1) * LANES], d_two, NT)
        tops.append(top)
        totals.append(jnp.sum(raised, axis=0, keepdims=True))
    stats_ref[...] = jnp.concatenate(tops + totals, axis=0)


def attention_kernel(
    rows,
    blocks, sources,
    near_ref, far_ref, low_ref, odd_ref, *refs
):
    more = len(sources) - 5
    attention_body(rows, blocks, sources, [near_ref, far_ref, low_ref, odd_ref, *refs[:more]], *refs[more:])


def attention_body(
    rows, blocks, sources, pool_refs,
    kv_t_ref, raised_ref, stats_ref, grads_ref, query_ref, datt_ref, datt_t_ref, wqkv_ref,
    back_ref, dkv_ref, att_ref, dq_ref,
    all_dkv_ref,
):
    width = NH * HEAD_SIZE
    own, count, pairs = rows.own, rows.pool, width // LANES
    pool = flags = 0.0
    for index, start, first, count_lines in sources:
        stack = pool_refs[index][...]
        shape = (rows.total - rows.pool, stack.shape[0])
        line = lax.broadcasted_iota(jnp.int32, shape, 0) - first
        source = lax.broadcasted_iota(jnp.int32, shape, 1) - start
        spot = line // blocks * (2 * blocks) + line % blocks
        given = (line >= 0) & (line < count_lines)
        pick_sum = jnp.where(given & (source == spot), 1.0, 0.0).astype(jnp.bfloat16)
        pick_flag = jnp.where(given & (source == spot + blocks), 1.0, 0.0).astype(jnp.bfloat16)
        pool = pool + DOT(pick_sum, stack, NN)
        flags = flags + DOT(pick_flag, stack[:, :own], NN)
    pool = pool.astype(jnp.bfloat16)
    pooled = jnp.where(flags > 0, 0.0, NEG_FILL)
    pooled2 = jnp.concatenate([pooled, pooled], axis=1)
    pool_kv = DOT(pool, wqkv_ref[:, width:], NN).astype(jnp.bfloat16)
    pool_kv_t = pool_kv.T
    query, d_att, d_att_t, stats = query_ref[...], datt_ref[...], datt_t_ref[...], stats_ref[...]

    for pair in range(pairs):
        lanes = slice(pair * LANES, (pair + 1) * LANES)
        value_lanes = slice(width + pair * LANES, width + (pair + 1) * LANES)
        heads = [slice(pair * LANES + h * HEAD_SIZE, pair * LANES + (h + 1) * HEAD_SIZE) for h in range(2)]
        q_two, d_two = two_heads(pair, own, query, d_att)
        scores = DOT(pool_kv[:, lanes], q_two, NT) + pooled2
        window_top = stats[pair : pair + 1]
        top = jnp.maximum(window_top, jnp.max(scores, axis=0, keepdims=True))
        raised = jnp.exp(scores - top)
        shrink = jnp.exp(window_top - top)
        scale = 1.0 / (stats[pairs + pair : pairs + pair + 1] * shrink + jnp.sum(raised, axis=0, keepdims=True))
        window_prob = raised_ref[pair * count : (pair + 1) * count] * (shrink * scale)
        pool_prob = raised * scale
        window_half, pool_half = window_prob.astype(jnp.bfloat16), pool_prob.astype(jnp.bfloat16)
        deltas = []
        for h, head in enumerate(heads):
            mine, value = slice(h * own, (h + 1) * own), slice(width + head.start, width + head.stop)
            part = DOT(kv_t_ref[value], window_half[:, mine], NN) + DOT(pool_kv_t[value], pool_half[:, mine], NN)
            part = part.astype(jnp.bfloat16)
            att_ref[head] = part
            deltas.append(
                jnp.sum(d_att_t[head].astype(jnp.float32) * part.astype(jnp.float32), axis=0, keepdims=True)
            )
        delta = jnp.concatenate(deltas, axis=1)
        window_grad = (window_prob * (grads_ref[pair * count : (pair + 1) * count] - delta)).astype(jnp.bfloat16)
        pool_grad = (pool_prob * (DOT(pool_kv[:, value_lanes], d_two, NT) - delta)).astype(jnp.bfloat16)
        score_grad = jnp.concatenate([window_grad, pool_grad], axis=0)
        prob_half = jnp.concatenate([window_half, pool_half], axis=0)
        all_dkv_ref[:, lanes] = DOT(score_grad, q_two, NN).astype(jnp.bfloat16)
        all_dkv_ref[:, value_lanes] = DOT(prob_half, d_two, NN).astype(jnp.bfloat16)
        for h, head in enumerate(heads):
            mine = slice(h * own, (h + 1) * own)
            part = DOT(kv_t_ref[head], window_grad[:, mine], NN) + DOT(pool_kv_t[head], pool_grad[:, mine], NN)
            dq_ref[head] = (part * SCALE).astype(jnp.bfloat16)
    back_ref[...] = DOT(all_dkv_ref[own:], wqkv_ref[:, width:], NT).astype(jnp.bfloat16)
    dkv_ref[...] = all_dkv_ref[:own]


def final_kernel(
    rows, mask_ref, tokens_ref, grad_ref, att_ref, dq_ref, dkv_ref, wqkv_ref, wout_ref, mixed_ref, own_ref
):
    width = NH * HEAD_SIZE
    flag = token_flags(rows, mask_ref, width)
    attended = (att_ref[...].T.astype(jnp.float32) * flag).astype(jnp.bfloat16)
    mixed = tokens_ref[...].astype(jnp.float32) + DOT(attended, wout_ref[...], NN)
    mixed_ref[...] = mixed.astype(jnp.bfloat16)
    own_ref[...] = (
        grad_ref[...].astype(jnp.float32)
        + DOT(dq_ref[...].T, wqkv_ref[:, :width], NT)
        + DOT(dkv_ref[...], wqkv_ref[:, width:], NT)
    )


def call(kernel, name, outs, scratch, flops, smem, *operands):
    vmem = pl.BlockSpec(memory_space=pltpu.VMEM)
    in_specs = [pl.BlockSpec(memory_space=pltpu.SMEM)] * smem + [vmem] * (len(operands) - smem)
    moved = sum(a.size * a.dtype.itemsize for a in operands)
    return pl.pallas_call(
        kernel,
        out_shape=tuple(jax.ShapeDtypeStruct(shape, dtype) for shape, dtype in outs),
        in_specs=in_specs,
        out_specs=tuple(vmem for _ in outs),
        scratch_shapes=[pltpu.VMEM(shape, dtype) for shape, dtype in scratch],
        compiler_params=pltpu.CompilerParams(vmem_limit_bytes=12 << 20),
        cost_estimate=pl.CostEstimate(flops=flops, transcendentals=0, bytes_accessed=moved),
        name=name,
    )(*operands)


def swap(name, value, axis, moves):
    with jax.named_scope(name):
        return lax.ppermute(value, axis, moves)


def local(tokens, w_qkv, w_out, block_mask, grad_out):
    tile_rows, tile_cols, width = tokens.shape
    count_y, count_x = lax.axis_size("gy"), lax.axis_size("gx")
    blocks = block_mask.shape[0] * block_mask.shape[1]
    rows = Rows(tile_rows, tile_cols, blocks * (count_y + count_x))
    own, side, edge, wide = rows.own, rows.side, rows.edge, rows.wide
    even_y, even_x = lax.axis_index("gy") % 2 == 0, lax.axis_index("gx") % 2 == 0
    flat_tokens = tokens.reshape(own, width)
    grad_flat = grad_out.reshape(own, width)
    half, full = jnp.bfloat16, jnp.float32

    macs = own * width * width
    bias = window_bias(rows, count_y, count_x)

    wide_tokens = lax.optimization_barrier(tokens.astype(full))
    sent_tokens = wide_tokens.astype(half)

    first = sent_tokens[:, :REACH].reshape(side, width)
    last = sent_tokens[:, tile_cols - REACH :].reshape(side, width)
    odd_send = jnp.where(even_x, first, last)
    odd_x = swap("r1_odd_columns", odd_send, "gx", pairs_odd(count_x, False))
    tokens_later, _ = lax.optimization_barrier((wide_tokens, odd_send))
    grouped = tokens_later.astype(full).reshape(
        tile_rows // TISSUE_BLOCK, TISSUE_BLOCK, tile_cols // TISSUE_BLOCK, TISSUE_BLOCK, width
    )
    sums = (jnp.sum(grouped, axis=(1, 3)) / TISSUE_BLOCK).reshape(blocks, width).astype(half)
    marks = jnp.broadcast_to(block_mask.reshape(blocks, 1), (blocks, width)).astype(half)
    mine = jnp.concatenate([sums, marks], axis=0)
    low_x = swap("r1_low_columns",
        jnp.concatenate([jnp.where(even_x, last, first), mine], axis=0), "gx", pairs_low(count_x)
    )
    row_pool = jnp.concatenate([mine, low_x[side:]], axis=0)
    *near_steps, last_step = steps_above(count_x, 2)
    for step in near_steps:
        got = swap(f"r1_far_columns_{step}", row_pool, "gx", pairs_far(count_x, step))
        row_pool = jnp.concatenate([row_pool, got], axis=0)
    got = swap(f"r1_far_columns_{last_step}", row_pool, "gx", pairs_far(count_x, last_step))
    spread = jnp.concatenate(
        [low_x[:side].reshape(tile_rows, REACH, width), sent_tokens, odd_x.reshape(tile_rows, REACH, width)], axis=1
    )
    top, bottom = spread[:REACH].reshape(edge, width), spread[tile_rows - REACH :].reshape(edge, width)
    low_y = swap("r1_low_rows",
        jnp.concatenate([jnp.where(even_y, bottom, top), mine], axis=0), "gy", pairs_low(count_y)
    )
    odd_y = swap("r1_odd_rows",
        jnp.concatenate([jnp.where(even_y, top, bottom), mine, low_y[edge:]], axis=0), "gy", pairs_odd(count_y, True)
    )
    row_lines, half_lines = count_x * blocks, row_pool.shape[0] // 2
    sources = [
        (0, 0, 0, half_lines),
        (1, 0, half_lines, half_lines),
        (0, 0, row_lines, blocks),
        (2, edge, row_lines + blocks, blocks),
        (3, edge, row_lines + 2 * blocks, 2 * blocks),
    ]
    more = []
    if count_y > 4:
        col_pool = jnp.concatenate([mine, low_y[edge:], odd_y[edge:]], axis=0)
    for step in steps_above(count_y // 2, 2):
        more.append(swap(f"r1_far_rows_{step}", col_pool, "gy", window_pairs(count_y, step)))
        col_pool = jnp.concatenate([col_pool, more[-1]], axis=0)
        lines = more[-1].shape[0] // 2
        sources.append((3 + len(more), 0, row_lines + lines, lines))
    count = rows.pool
    pairs = width // LANES
    query, d_att, d_att_t, kv_t, raised, stats, grads = call(
        functools.partial(window_kernel, rows), "window",
        [
            ((own, width), half), ((own, width), half), ((width, own), half), ((2 * width, count), half),
            ((pairs * count, 2 * own), full), ((2 * pairs, 2 * own), full), ((pairs * count, 2 * own), full),
        ],
        [((count, width), half)],
        22 * macs, 1, block_mask, flat_tokens, low_x, odd_x, low_y, odd_y, bias, grad_flat, w_qkv, w_out,
    )
    back, d_kv, att, d_query = call(
        functools.partial(attention_kernel, rows, blocks, sources), "attention",
        [((rows.total - own, width), half), ((own, 2 * width), half), ((width, own), half), ((width, own), half)],
        [((rows.total, 2 * width), half)],
        26 * macs, 0, row_pool, got, low_y, odd_y, *more, kv_t, raised, stats, grads, query, d_att, d_att_t, w_qkv,
    )

    def piece(start, count):
        return back[start - own : start - own + count]

    def fold(grads, got):
        return (grads.astype(full) + got.astype(full)).astype(half)

    row_grad = piece(rows.pool, count_x * blocks)
    col_grad = piece(rows.pool + count_x * blocks, count_y * blocks)
    for step in reversed(steps_above(count_y // 2, 2)):
        middle = col_grad.shape[0] // 2
        got = swap(f"r2_far_rows_{step}", col_grad[middle:], "gy", window_pairs(count_y, step))
        col_grad = fold(col_grad[:middle], got)
    odd_rows = swap(
        "r2_odd_rows",
        jnp.concatenate([piece(rows.odd_y, edge), col_grad[2 * blocks :]], axis=0),
        "gy",
        pairs_odd(count_y, True),
    )
    col_grad = fold(col_grad[: 2 * blocks], odd_rows[edge:])
    low_rows = swap(
        "r2_low_rows", jnp.concatenate([piece(rows.low_y, edge), col_grad[blocks:]], axis=0), "gy", pairs_low(count_y)
    )
    for step in reversed(steps_above(count_x, 2)):
        if step == 2:
            row_grad, low_rows = lax.optimization_barrier((row_grad, low_rows))
        middle = row_grad.shape[0] // 2
        got = swap(f"r2_far_columns_{step}", row_grad[middle:], "gx", pairs_far(count_x, step))
        row_grad = fold(row_grad[:middle], got)
    att, row_grad = lax.optimization_barrier((att, row_grad))
    mixed, own_back = call(
        functools.partial(final_kernel, rows), "final", [((own, width), half), ((own, width), full)],
        [], 8 * macs, 1, block_mask, flat_tokens, grad_flat, att, d_query, d_kv, w_qkv, w_out,
    )
    col_grad = fold(col_grad[:blocks], low_rows[edge:])
    odd_rows = odd_rows[:edge].astype(full).reshape(REACH, wide, width)
    low_rows = low_rows[:edge].astype(full).reshape(REACH, wide, width)
    at_top, at_bottom = jnp.where(even_y, odd_rows, low_rows), jnp.where(even_y, low_rows, odd_rows)
    room = tile_rows - REACH

    def lines(start, stop):
        top, bottom = at_top[:, start:stop], at_bottom[:, start:stop]
        return jnp.pad(top, ((0, room), (0, 0), (0, 0))) + jnp.pad(bottom, ((room, 0), (0, 0), (0, 0)))

    odd_side = piece(rows.odd_x, side).astype(full) + lines(wide - REACH, wide).reshape(side, width)
    odd_got = swap("r2_odd_columns", odd_side.astype(half), "gx", pairs_odd(count_x, False))
    low_side = piece(rows.low_x, side).astype(full) + lines(0, REACH).reshape(side, width)
    room = tile_cols - REACH
    d_tokens = own_back.reshape(tile_rows, tile_cols, width) + jnp.pad(
        at_top[:, REACH : REACH + tile_cols], ((0, tile_rows - REACH), (0, 0), (0, 0))
    )
    d_tokens = d_tokens + jnp.pad(at_bottom[:, REACH : REACH + tile_cols], ((tile_rows - REACH, 0), (0, 0), (0, 0)))

    def columns(got, at_first):
        got = got.astype(full).reshape(tile_rows, REACH, width)
        first, last = jnp.pad(got, ((0, 0), (0, room), (0, 0))), jnp.pad(got, ((0, 0), (room, 0), (0, 0)))
        return jnp.where(at_first, first, last)

    d_tokens = d_tokens + columns(odd_got, even_x)
    low_got = swap(
        "r2_low_columns",
        jnp.concatenate([low_side.astype(half), row_grad[blocks:]], axis=0),
        "gx",
        pairs_low(count_x),
    )
    low_got, d_tokens = lax.optimization_barrier((low_got, d_tokens))
    block_grad = row_grad[:blocks].astype(full) + low_got[side:].astype(full) + col_grad.astype(full)
    d_tokens = d_tokens + columns(low_got[:side], ~even_x)
    shaped = (block_grad / TISSUE_BLOCK).reshape(tile_rows // TISSUE_BLOCK, tile_cols // TISSUE_BLOCK, width)
    d_tokens = d_tokens + jnp.repeat(jnp.repeat(shaped, TISSUE_BLOCK, 0), TISSUE_BLOCK, 1)
    return mixed.reshape(tile_rows, tile_cols, width), d_tokens.astype(half)


def solution(mesh):
    placed = (P("gy", "gx", None), P(), P(), P("gy", "gx"), P("gy", "gx", None))
    return jax.shard_map(
        local,
        mesh=mesh,
        in_specs=placed,
        out_specs=(P("gy", "gx", None), P("gy", "gx", None)),
        check_vma=False,
    )
```

```python
import functools

import jax
import jax.numpy as jnp
import numpy as np
from jax import lax
from jax.experimental import pallas as pl
from jax.experimental.pallas import tpu as pltpu
from jax.sharding import PartitionSpec as P

NH = 6
HEAD_SIZE = 64
KS = 7
TISSUE_BLOCK = 8
REACH = KS // 2
NEG_FILL = -1e30
LANES = 128
ALIGN = 16
FAR = -1000


def pairs_low(count):
    return [(i, i ^ 1) for i in range(count)]


def pairs_odd(count, wrap):
    moves = []
    for i in range(count):
        j = (i + 1) % count if i % 2 else (i - 1) % count
        if wrap or abs(i - j) == 1:
            moves.append((i, j))
    return moves


def pairs_far(count, step):
    return [(i, i ^ step) for i in range(count)]


def window_pairs(count, step):
    moves = []
    for i in range(count):
        group, side = divmod((i - 1) % count, 2)
        moves.append((i, (2 * (group ^ step) + 1 + side) % count))
    return moves


def steps_above(count, first):
    steps = []
    while first < count:
        steps.append(first)
        first *= 2
    return steps


def padded(count, unit=ALIGN):
    return -(-count // unit) * unit


class Rows:
    def __init__(self, tile_rows, tile_cols, pooled):
        self.tile_rows, self.tile_cols = tile_rows, tile_cols
        self.wide = tile_cols + 2 * REACH
        self.own = tile_rows * tile_cols
        self.side = tile_rows * REACH
        self.edge = REACH * self.wide
        self.low_x = self.own
        self.odd_x = self.low_x + padded(self.side)
        self.low_y = self.odd_x + padded(self.side)
        self.odd_y = self.low_y + padded(self.edge)
        self.pool = self.odd_y + padded(self.edge)
        self.pooled = pooled
        self.used = self.pool + pooled
        self.total = padded(self.used, LANES)


def places(rows):
    tile_rows, tile_cols = rows.tile_rows, rows.tile_cols
    place = np.full((2, 2, rows.total, 2), FAR, np.int32)

    def grid(first, second):
        return np.stack(np.meshgrid(np.asarray(first), np.asarray(second), indexing="ij"), -1).reshape(-1, 2)

    before, own_cols, after = np.arange(-REACH, 0), np.arange(tile_cols), tile_cols + np.arange(REACH)
    above, own_rows, below = np.arange(-REACH, 0), np.arange(tile_rows), tile_rows + np.arange(REACH)
    for odd_y in range(2):
        for odd_x in range(2):
            low_cols, odd_cols = (before, after) if odd_x else (after, before)
            low_rows, odd_rows = (above, below) if odd_y else (below, above)
            wide_cols = np.concatenate([low_cols, own_cols, odd_cols])
            spot = place[odd_y, odd_x]
            spot[: rows.own] = grid(own_rows, own_cols)
            spot[rows.low_x : rows.low_x + rows.side] = grid(own_rows, low_cols)
            spot[rows.odd_x : rows.odd_x + rows.side] = grid(own_rows, odd_cols)
            spot[rows.low_y : rows.low_y + rows.edge] = grid(low_rows, wide_cols)
            spot[rows.odd_y : rows.odd_y + rows.edge] = grid(odd_rows, wide_cols)
    return place


def window_bias(rows, count_y, count_x):
    iy, ix = lax.axis_index("gy"), lax.axis_index("gx")
    table = jnp.asarray(places(rows))
    key = table[iy % 2, ix % 2]
    key_row, key_col = key[:, :1], key[:, 1:]
    token = np.arange(rows.own)[None, :]
    near = (jnp.abs(key_row - token // rows.tile_cols) <= REACH) & (jnp.abs(key_col - token % rows.tile_cols) <= REACH)
    row, col = iy * rows.tile_rows + key_row, ix * rows.tile_cols + key_col
    inside = (row >= 0) & (row < count_y * rows.tile_rows) & (col >= 0) & (col < count_x * rows.tile_cols)
    return jnp.where(near & inside, 0.0, NEG_FILL).astype(jnp.float32)


DOT = functools.partial(lax.dot_general, preferred_element_type=jnp.float32)
NN = (((1,), (0,)), ((), ()))
NT = (((1,), (1,)), ((), ()))
SCALE = HEAD_SIZE**-0.5


def token_flags(rows, mask_ref, width):
    token = lax.broadcasted_iota(jnp.int32, (rows.own, width), 0)
    block_cols = rows.tile_cols // TISSUE_BLOCK
    block = token // (rows.tile_cols * TISSUE_BLOCK) * block_cols + token % rows.tile_cols // TISSUE_BLOCK
    flag = jnp.zeros((rows.own, width), jnp.float32)
    for b in range(mask_ref.shape[0] * mask_ref.shape[1]):
        value = mask_ref[b // block_cols, b % block_cols].astype(jnp.float32)
        flag = jnp.where(block == b, value, flag)
    return flag


def gather_kernel(rows, blocks, mask_ref, tokens_ref, sent_ref, mine_ref):
    tokens = tokens_ref[...]
    sent_ref[...] = tokens
    shape = (blocks, rows.own)
    line, token = lax.broadcasted_iota(jnp.int32, shape, 0), lax.broadcasted_iota(jnp.int32, shape, 1)
    block_cols = rows.tile_cols // TISSUE_BLOCK
    block = token // (rows.tile_cols * TISSUE_BLOCK) * block_cols + token % rows.tile_cols // TISSUE_BLOCK
    pick = jnp.where(block == line, 1.0 / TISSUE_BLOCK, 0.0).astype(jnp.bfloat16)
    sums = DOT(pick, tokens, NN)
    row = lax.broadcasted_iota(jnp.int32, sums.shape, 0)
    marks = jnp.zeros_like(sums)
    for b in range(blocks):
        r, c = b // block_cols, b % block_cols
        marks = jnp.where(row == b, mask_ref[r : r + 1, c : c + 1].astype(jnp.float32), marks)
    mine_ref[...] = jnp.concatenate([sums, marks], axis=0).astype(jnp.bfloat16)


def two_heads(pair, own, query, d_att):
    low = lax.broadcasted_iota(jnp.int32, (own, LANES), 1) < HEAD_SIZE
    none = jnp.zeros((own, LANES), jnp.bfloat16)

    def stack(field):
        part = field[:, pair * LANES : (pair + 1) * LANES]
        return jnp.concatenate([jnp.where(low, part, none), jnp.where(low, none, part)], axis=0)

    return stack(query), stack(d_att)


def window_kernel(
    rows,
    mask_ref, tokens_ref, low_x_ref, odd_x_ref, low_y_ref, odd_y_ref, bias_ref, grad_ref, wqkv_ref, wout_ref,
    query_ref, datt_ref, datt_t_ref, kv_t_ref, raised_ref, stats_ref, grads_ref,
    x_ref,
):
    width = NH * HEAD_SIZE
    own, count = rows.own, rows.pool
    tokens = tokens_ref[...]
    x_ref[...] = jnp.zeros_like(x_ref)
    x_ref[:own] = tokens
    for start, ref, size in (
        (rows.low_x, low_x_ref, rows.side),
        (rows.odd_x, odd_x_ref, rows.side),
        (rows.low_y, low_y_ref, rows.edge),
        (rows.odd_y, odd_y_ref, rows.edge),
    ):
        x_ref[start : start + size] = ref[:size]
    query = DOT(tokens, wqkv_ref[:, :width], NN).astype(jnp.bfloat16).astype(jnp.float32) * SCALE
    query = query.astype(jnp.bfloat16)
    query_ref[...] = query
    flag = token_flags(rows, mask_ref, width)
    d_att = (DOT(grad_ref[...], wout_ref[...], NT) * flag).astype(jnp.bfloat16)
    datt_ref[...] = d_att
    datt_t_ref[...] = d_att.T
    kv = DOT(x_ref[...], wqkv_ref[:, width:], NN).astype(jnp.bfloat16)
    kv_t_ref[...] = kv.T
    bias = bias_ref[:count]
    bias2 = jnp.concatenate([bias, bias], axis=1)
    tops, totals = [], []
    for pair in range(width // LANES):
        lanes = slice(pair * LANES, (pair + 1) * LANES)
        q_two, d_two = two_heads(pair, own, query, d_att)
        scores = DOT(kv[:, lanes], q_two, NT) + bias2
        top = jnp.max(scores, axis=0, keepdims=True)
        raised = jnp.exp(scores - top)
        raised_ref[pair * count : (pair + 1) * count] = raised
        grads_ref[pair * count : (pair + 1) * count] = DOT(kv[:, width + pair * LANES : width + (pair + 1) * LANES], d_two, NT)
        tops.append(top)
        totals.append(jnp.sum(raised, axis=0, keepdims=True))
    stats_ref[...] = jnp.concatenate(tops + totals, axis=0)


def attention_kernel(
    rows,
    blocks, sources,
    near_ref, far_ref, low_ref, odd_ref, *refs
):
    more = len(sources) - 5
    attention_body(rows, blocks, sources, [near_ref, far_ref, low_ref, odd_ref, *refs[:more]], *refs[more:])


def attention_body(
    rows, blocks, sources, pool_refs,
    kv_t_ref, raised_ref, stats_ref, grads_ref, query_ref, datt_ref, datt_t_ref, wqkv_ref,
    back_ref, dkv_ref, att_ref, dq_ref,
    all_dkv_ref,
):
    width = NH * HEAD_SIZE
    own, count, pairs = rows.own, rows.pool, width // LANES
    pool = flags = 0.0
    for index, start, first, count_lines in sources:
        stack = pool_refs[index][...]
        shape = (rows.total - rows.pool, stack.shape[0])
        line = lax.broadcasted_iota(jnp.int32, shape, 0) - first
        source = lax.broadcasted_iota(jnp.int32, shape, 1) - start
        spot = line // blocks * (2 * blocks) + line % blocks
        given = (line >= 0) & (line < count_lines)
        pick_sum = jnp.where(given & (source == spot), 1.0, 0.0).astype(jnp.bfloat16)
        pick_flag = jnp.where(given & (source == spot + blocks), 1.0, 0.0).astype(jnp.bfloat16)
        pool = pool + DOT(pick_sum, stack, NN)
        flags = flags + DOT(pick_flag, stack[:, :own], NN)
    pool = pool.astype(jnp.bfloat16)
    pooled = jnp.where(flags > 0, 0.0, NEG_FILL)
    pooled2 = jnp.concatenate([pooled, pooled], axis=1)
    pool_kv = DOT(pool, wqkv_ref[:, width:], NN).astype(jnp.bfloat16)
    pool_kv_t = pool_kv.T
    query, d_att, d_att_t, stats = query_ref[...], datt_ref[...], datt_t_ref[...], stats_ref[...]

    for pair in range(pairs):
        lanes = slice(pair * LANES, (pair + 1) * LANES)
        value_lanes = slice(width + pair * LANES, width + (pair + 1) * LANES)
        heads = [slice(pair * LANES + h * HEAD_SIZE, pair * LANES + (h + 1) * HEAD_SIZE) for h in range(2)]
        q_two, d_two = two_heads(pair, own, query, d_att)
        scores = DOT(pool_kv[:, lanes], q_two, NT) + pooled2
        window_top = stats[pair : pair + 1]
        top = jnp.maximum(window_top, jnp.max(scores, axis=0, keepdims=True))
        raised = jnp.exp(scores - top)
        shrink = jnp.exp(window_top - top)
        scale = 1.0 / (stats[pairs + pair : pairs + pair + 1] * shrink + jnp.sum(raised, axis=0, keepdims=True))
        window_prob = raised_ref[pair * count : (pair + 1) * count] * (shrink * scale)
        pool_prob = raised * scale
        window_half, pool_half = window_prob.astype(jnp.bfloat16), pool_prob.astype(jnp.bfloat16)
        deltas = []
        for h, head in enumerate(heads):
            mine, value = slice(h * own, (h + 1) * own), slice(width + head.start, width + head.stop)
            part = DOT(kv_t_ref[value], window_half[:, mine], NN) + DOT(pool_kv_t[value], pool_half[:, mine], NN)
            part = part.astype(jnp.bfloat16)
            att_ref[head] = part
            deltas.append(
                jnp.sum(d_att_t[head].astype(jnp.float32) * part.astype(jnp.float32), axis=0, keepdims=True)
            )
        delta = jnp.concatenate(deltas, axis=1)
        window_grad = (window_prob * (grads_ref[pair * count : (pair + 1) * count] - delta)).astype(jnp.bfloat16)
        pool_grad = (pool_prob * (DOT(pool_kv[:, value_lanes], d_two, NT) - delta)).astype(jnp.bfloat16)
        score_grad = jnp.concatenate([window_grad, pool_grad], axis=0)
        prob_half = jnp.concatenate([window_half, pool_half], axis=0)
        all_dkv_ref[:, lanes] = DOT(score_grad, q_two, NN).astype(jnp.bfloat16)
        all_dkv_ref[:, value_lanes] = DOT(prob_half, d_two, NN).astype(jnp.bfloat16)
        for h, head in enumerate(heads):
            mine = slice(h * own, (h + 1) * own)
            part = DOT(kv_t_ref[head], window_grad[:, mine], NN) + DOT(pool_kv_t[head], pool_grad[:, mine], NN)
            dq_ref[head] = (part * SCALE).astype(jnp.bfloat16)
    back_ref[...] = DOT(all_dkv_ref[own:], wqkv_ref[:, width:], NT).astype(jnp.bfloat16)
    dkv_ref[...] = all_dkv_ref[:own]


def final_kernel(
    rows, mask_ref, tokens_ref, grad_ref, att_ref, dq_ref, dkv_ref, wqkv_ref, wout_ref, mixed_ref, own_ref
):
    width = NH * HEAD_SIZE
    flag = token_flags(rows, mask_ref, width)
    attended = (att_ref[...].T.astype(jnp.float32) * flag).astype(jnp.bfloat16)
    mixed = tokens_ref[...].astype(jnp.float32) + DOT(attended, wout_ref[...], NN)
    mixed_ref[...] = mixed.astype(jnp.bfloat16)
    own_ref[...] = (
        grad_ref[...].astype(jnp.float32)
        + DOT(dq_ref[...].T, wqkv_ref[:, :width], NT)
        + DOT(dkv_ref[...], wqkv_ref[:, width:], NT)
    )


def call(kernel, name, outs, scratch, flops, smem, *operands):
    vmem = pl.BlockSpec(memory_space=pltpu.VMEM)
    in_specs = [pl.BlockSpec(memory_space=pltpu.SMEM)] * smem + [vmem] * (len(operands) - smem)
    moved = sum(a.size * a.dtype.itemsize for a in operands)
    return pl.pallas_call(
        kernel,
        out_shape=tuple(jax.ShapeDtypeStruct(shape, dtype) for shape, dtype in outs),
        in_specs=in_specs,
        out_specs=tuple(vmem for _ in outs),
        scratch_shapes=[pltpu.VMEM(shape, dtype) for shape, dtype in scratch],
        compiler_params=pltpu.CompilerParams(vmem_limit_bytes=12 << 20),
        cost_estimate=pl.CostEstimate(flops=flops, transcendentals=0, bytes_accessed=moved),
        name=name,
    )(*operands)


def swap(name, value, axis, moves):
    with jax.named_scope(name):
        return lax.ppermute(value, axis, moves)


def local(tokens, w_qkv, w_out, block_mask, grad_out):
    tile_rows, tile_cols, width = tokens.shape
    count_y, count_x = lax.axis_size("gy"), lax.axis_size("gx")
    blocks = block_mask.shape[0] * block_mask.shape[1]
    rows = Rows(tile_rows, tile_cols, blocks * (count_y + count_x))
    own, side, edge, wide = rows.own, rows.side, rows.edge, rows.wide
    even_y, even_x = lax.axis_index("gy") % 2 == 0, lax.axis_index("gx") % 2 == 0
    flat_tokens = tokens.reshape(own, width)
    grad_flat = grad_out.reshape(own, width)
    half, full = jnp.bfloat16, jnp.float32

    macs = own * width * width
    bias = window_bias(rows, count_y, count_x)

    sent_tokens, mine = call(
        functools.partial(gather_kernel, rows, blocks), "gather", [((own, width), half), ((2 * blocks, width), half)],
        [], 1, 0, block_mask, flat_tokens,
    )
    sent_tokens = sent_tokens.reshape(tile_rows, tile_cols, width)

    first = sent_tokens[:, :REACH].reshape(side, width)
    last = sent_tokens[:, tile_cols - REACH :].reshape(side, width)
    odd_send = jnp.where(even_x, first, last)
    odd_x = swap("r1_odd_columns", odd_send, "gx", pairs_odd(count_x, False))
    mine, _ = lax.optimization_barrier((mine, odd_send))
    low_x = swap("r1_low_columns",
        jnp.concatenate([jnp.where(even_x, last, first), mine], axis=0), "gx", pairs_low(count_x)
    )
    row_pool = jnp.concatenate([mine, low_x[side:]], axis=0)
    *near_steps, last_step = steps_above(count_x, 2)
    for step in near_steps:
        got = swap(f"r1_far_columns_{step}", row_pool, "gx", pairs_far(count_x, step))
        row_pool = jnp.concatenate([row_pool, got], axis=0)
    got = swap(f"r1_far_columns_{last_step}", row_pool, "gx", pairs_far(count_x, last_step))
    spread = jnp.concatenate(
        [low_x[:side].reshape(tile_rows, REACH, width), sent_tokens, odd_x.reshape(tile_rows, REACH, width)], axis=1
    )
    top, bottom = spread[:REACH].reshape(edge, width), spread[tile_rows - REACH :].reshape(edge, width)
    low_y = swap("r1_low_rows",
        jnp.concatenate([jnp.where(even_y, bottom, top), mine], axis=0), "gy", pairs_low(count_y)
    )
    odd_y = swap("r1_odd_rows",
        jnp.concatenate([jnp.where(even_y, top, bottom), mine, low_y[edge:]], axis=0), "gy", pairs_odd(count_y, True)
    )
    row_lines, half_lines = count_x * blocks, row_pool.shape[0] // 2
    sources = [
        (0, 0, 0, half_lines),
        (1, 0, half_lines, half_lines),
        (0, 0, row_lines, blocks),
        (2, edge, row_lines + blocks, blocks),
        (3, edge, row_lines + 2 * blocks, 2 * blocks),
    ]
    more = []
    if count_y > 4:
        col_pool = jnp.concatenate([mine, low_y[edge:], odd_y[edge:]], axis=0)
    for step in steps_above(count_y // 2, 2):
        more.append(swap(f"r1_far_rows_{step}", col_pool, "gy", window_pairs(count_y, step)))
        col_pool = jnp.concatenate([col_pool, more[-1]], axis=0)
        lines = more[-1].shape[0] // 2
        sources.append((3 + len(more), 0, row_lines + lines, lines))
    count = rows.pool
    pairs = width // LANES
    query, d_att, d_att_t, kv_t, raised, stats, grads = call(
        functools.partial(window_kernel, rows), "window",
        [
            ((own, width), half), ((own, width), half), ((width, own), half), ((2 * width, count), half),
            ((pairs * count, 2 * own), full), ((2 * pairs, 2 * own), full), ((pairs * count, 2 * own), full),
        ],
        [((count, width), half)],
        22 * macs, 1, block_mask, flat_tokens, low_x, odd_x, low_y, odd_y, bias, grad_flat, w_qkv, w_out,
    )
    back, d_kv, att, d_query = call(
        functools.partial(attention_kernel, rows, blocks, sources), "attention",
        [((rows.total - own, width), half), ((own, 2 * width), half), ((width, own), half), ((width, own), half)],
        [((rows.total, 2 * width), half)],
        26 * macs, 0, row_pool, got, low_y, odd_y, *more, kv_t, raised, stats, grads, query, d_att, d_att_t, w_qkv,
    )

    def piece(start, count):
        return back[start - own : start - own + count]

    def fold(grads, got):
        return (grads.astype(full) + got.astype(full)).astype(half)

    row_grad = piece(rows.pool, count_x * blocks)
    col_grad = piece(rows.pool + count_x * blocks, count_y * blocks)
    for step in reversed(steps_above(count_y // 2, 2)):
        middle = col_grad.shape[0] // 2
        got = swap(f"r2_far_rows_{step}", col_grad[middle:], "gy", window_pairs(count_y, step))
        col_grad = fold(col_grad[:middle], got)
    odd_rows = swap(
        "r2_odd_rows",
        jnp.concatenate([piece(rows.odd_y, edge), col_grad[2 * blocks :]], axis=0),
        "gy",
        pairs_odd(count_y, True),
    )
    col_grad = fold(col_grad[: 2 * blocks], odd_rows[edge:])
    low_rows = swap(
        "r2_low_rows", jnp.concatenate([piece(rows.low_y, edge), col_grad[blocks:]], axis=0), "gy", pairs_low(count_y)
    )
    for step in reversed(steps_above(count_x, 2)):
        if step == 2:
            row_grad, low_rows = lax.optimization_barrier((row_grad, low_rows))
        middle = row_grad.shape[0] // 2
        got = swap(f"r2_far_columns_{step}", row_grad[middle:], "gx", pairs_far(count_x, step))
        row_grad = fold(row_grad[:middle], got)
    att, row_grad = lax.optimization_barrier((att, row_grad))
    mixed, own_back = call(
        functools.partial(final_kernel, rows), "final", [((own, width), half), ((own, width), full)],
        [], 8 * macs, 1, block_mask, flat_tokens, grad_flat, att, d_query, d_kv, w_qkv, w_out,
    )
    col_grad = fold(col_grad[:blocks], low_rows[edge:])
    odd_rows = odd_rows[:edge].astype(full).reshape(REACH, wide, width)
    low_rows = low_rows[:edge].astype(full).reshape(REACH, wide, width)
    at_top, at_bottom = jnp.where(even_y, odd_rows, low_rows), jnp.where(even_y, low_rows, odd_rows)
    room = tile_rows - REACH

    def lines(start, stop):
        top, bottom = at_top[:, start:stop], at_bottom[:, start:stop]
        return jnp.pad(top, ((0, room), (0, 0), (0, 0))) + jnp.pad(bottom, ((room, 0), (0, 0), (0, 0)))

    odd_side = piece(rows.odd_x, side).astype(full) + lines(wide - REACH, wide).reshape(side, width)
    odd_got = swap("r2_odd_columns", odd_side.astype(half), "gx", pairs_odd(count_x, False))
    low_side = piece(rows.low_x, side).astype(full) + lines(0, REACH).reshape(side, width)
    room = tile_cols - REACH
    d_tokens = own_back.reshape(tile_rows, tile_cols, width) + jnp.pad(
        at_top[:, REACH : REACH + tile_cols], ((0, tile_rows - REACH), (0, 0), (0, 0))
    )
    d_tokens = d_tokens + jnp.pad(at_bottom[:, REACH : REACH + tile_cols], ((tile_rows - REACH, 0), (0, 0), (0, 0)))

    def columns(got, at_first):
        got = got.astype(full).reshape(tile_rows, REACH, width)
        first, last = jnp.pad(got, ((0, 0), (0, room), (0, 0))), jnp.pad(got, ((0, 0), (room, 0), (0, 0)))
        return jnp.where(at_first, first, last)

    d_tokens = d_tokens + columns(odd_got, even_x)
    low_got = swap(
        "r2_low_columns",
        jnp.concatenate([low_side.astype(half), row_grad[blocks:]], axis=0),
        "gx",
        pairs_low(count_x),
    )
    low_got, d_tokens = lax.optimization_barrier((low_got, d_tokens))
    block_grad = row_grad[:blocks].astype(full) + low_got[side:].astype(full) + col_grad.astype(full)
    d_tokens = d_tokens + columns(low_got[:side], ~even_x)
    shaped = (block_grad / TISSUE_BLOCK).reshape(tile_rows // TISSUE_BLOCK, tile_cols // TISSUE_BLOCK, width)
    d_tokens = d_tokens + jnp.repeat(jnp.repeat(shaped, TISSUE_BLOCK, 0), TISSUE_BLOCK, 1)
    return mixed.reshape(tile_rows, tile_cols, width), d_tokens.astype(half)


def solution(mesh):
    placed = (P("gy", "gx", None), P(), P(), P("gy", "gx"), P("gy", "gx", None))
    return jax.shard_map(
        local,
        mesh=mesh,
        in_specs=placed,
        out_specs=(P("gy", "gx", None), P("gy", "gx", None)),
        check_vma=False,
    )
```
